32 devices in a mesh: grp: 2 (over y), blk: 4 (over z), head: 4 (over x, core).
Axes of the slice: x: 2, y: 2, z: 4, core: 2. Of those that a mesh axis runs over, the one named last changes fastest.
Arguments:
- query: bfloat16 [2048, 512], P(('grp', 'blk', 'head')), parts along dimension 0, may hold values from -128 to 128
- keys: bfloat16 [2048, 512], P(('grp', 'blk', 'head')), parts along dimension 0, may hold values from -8 to 8
- values: bfloat16 [2048, 512], P(('grp', 'blk', 'head')), parts along dimension 0, may hold values from -6 to 6
- grad_out: bfloat16 [2048, 512], P(('grp', 'blk', 'head')), parts along dimension 0, may hold values from -6 to 6
- valid: int32 [64], P('grp'), parts along dimension 0, may hold values from 16 to 32, as said below
- views: int32 [64], P('grp'), parts along dimension 0, may hold values from 0 to 1
- cross_bias: float32 [8], replicated, may hold values from -2 to 2
Outputs:
- grad_query: float32 [2048, 512], P(('grp', 'blk', 'head')), parts along dimension 0
- grad_keys: float32 [2048, 512], P(('grp', 'blk', 'head')), parts along dimension 0
- grad_values: float32 [2048, 512], P(('grp', 'blk', 'head')), parts along dimension 0
The draws below stay inside these ranges and needn't reach their ends.
There are 2 independent parts, one for each index of `grp`. The reference program is written for one: setup_inputs(seed, part) draws one part's arguments, and reference() takes and returns one part's arrays. A program takes and returns all parts, laid end to end along the dimension named above; an argument that names none is the same for every part. Nothing has to cross between parts.
Inputs may be any that keep to these rules, and one draw needn't show every extreme that they name: `valid`: every frame has at least half of its slots live, and some frame has all 32 live.
All inputs are finite; a program needn't handle non-finite values.
Results may differ from the reference program's by a relative error of at most 0.025.
Values may be sent and summed in bfloat16 or wider, within the bound.
A program may use at most 64 MiB of HBM per device.

```python
import jax
import jax.numpy as jnp
from jax import lax

HEADS = 8
HD = 64
FRAME = 32
TOK_DEV = 64
FRAMES = 32
TOKENS = 1024
N_HEAD = 4


def paired_fields(key):
    shape = (TOKENS, HEADS * HD)
    key_scale = 128.0 / HD
    key_base = jnp.clip(jax.random.normal(jax.random.fold_in(key, 11), shape, jnp.float32), -4.0, 4.0)
    key_part = key_base * key_scale
    query_part = jnp.clip(jax.random.normal(jax.random.fold_in(key, 12), shape, jnp.float32), -4.0, 4.0)
    return (query_part, key_part)


def draw_query(key, part):
    return paired_fields(key)[0].astype(jnp.bfloat16)


def draw_keys(key, part):
    return paired_fields(key)[1].astype(jnp.bfloat16)


def draw_valid(key, part):
    counts = jax.random.randint(jax.random.fold_in(key, 13), (FRAMES,), FRAME // 2, FRAME + 1, dtype=jnp.int32)
    return jnp.where(jnp.arange(FRAMES) == 0, FRAME, counts).astype(jnp.int32)


def with_ends(drawn, own_key, least, high):
    longest = drawn.shape.index(max(drawn.shape))
    spots = []
    for shift in (0, 1):
        where = [jax.random.randint(jax.random.fold_in(own_key, axis), (), 0, length) for axis, length in enumerate(drawn.shape)]
        where[longest] = (where[longest] + shift) % drawn.shape[longest]
        spots.append(tuple(where))
    return drawn.at[spots[0]].set(least).at[spots[1]].set(high)


def shard_levels(rng, dims, cuts, low, high):
    gain, own = 1.0, jax.random.fold_in(rng, 6)
    for dim, shards_of in cuts:
        steps = jnp.exp(jax.random.uniform(jax.random.fold_in(own, dim), (shards_of,), jnp.float32, low / len(cuts), high / len(cuts)))
        gain = gain * jnp.repeat(steps, dims[dim] // shards_of).reshape([-1 if axis == dim else 1 for axis in range(len(dims))])
    return gain


def scatter_about(stream_key, shape, deviation, limit, shards=(), kind=jnp.bfloat16):
    loudness = shard_levels(stream_key, shape, shards, -0.22, 0.18) if shards else 1.0
    values = jax.random.normal(stream_key, shape, jnp.float32) * deviation * loudness
    return jnp.minimum(jnp.maximum(values, -limit), limit).astype(kind)


def setup_inputs(seed: int = 0, part: int = 0) -> dict:
    key_of = jax.random.split(jax.random.key(seed), 8)
    part_keys = jax.random.split(jax.random.fold_in(key_of[7], part), 8)
    query = draw_query(jax.random.fold_in(jax.random.fold_in(key_of[7], part), 71), part)
    keys = draw_keys(jax.random.fold_in(jax.random.fold_in(key_of[7], part), 71), part)
    values = scatter_about(part_keys[2], (TOKENS, HEADS * HD), 1.0, 6.0, ((0, 16),))
    grad_out = scatter_about(part_keys[3], (TOKENS, HEADS * HD), 1.0, 6.0, ((0, 16),))
    valid = draw_valid(jax.random.fold_in(jax.random.fold_in(key_of[7], part), 71), part)
    views = with_ends(jax.random.randint(part_keys[5], (FRAMES,), 0, 2), jax.random.fold_in(part_keys[5], 1), 0, 1).astype(jnp.int32)
    cross_bias = jnp.clip(jax.random.uniform(key_of[6], (HEADS,), jnp.float32, -2.0, 2.0), -2.0, 2.0)
    return dict(query=query, keys=keys, values=values, grad_out=grad_out, valid=valid, views=views, cross_bias=cross_bias)


neg_large = -1.0e30


def reference(query, keys, values, grad_out, valid, views, cross_bias):
    tokens = jnp.arange(TOKENS, dtype=jnp.int32)
    frames = tokens // FRAME
    live = (tokens % FRAME) < valid[frames]
    labels = views[frames]
    block_len = N_HEAD * TOK_DEV
    count = TOKENS // block_len

    def per_head(head):
        q_head = lax.dynamic_slice_in_dim(query, head * HD, HD, 1)
        k_head = lax.dynamic_slice_in_dim(keys, head * HD, HD, 1)
        v_head = lax.dynamic_slice_in_dim(values, head * HD, HD, 1)
        g_head = lax.dynamic_slice_in_dim(grad_out, head * HD, HD, 1)
        bias = cross_bias[head]

        def one(carry, index):
            dk_acc, dv_acc = carry
            start = (index * block_len).astype(jnp.int32)
            q_part = lax.dynamic_slice_in_dim(q_head, start, block_len, 0)
            g_part = lax.dynamic_slice_in_dim(g_head, start, block_len, 0)
            q_label = lax.dynamic_slice_in_dim(labels, start, block_len, 0)
            cross = (q_label[:, None] != labels[None, :]).astype(jnp.float32)
            logits = jnp.dot(q_part, k_head.T, preferred_element_type=jnp.float32) * 0.125 + bias * cross
            logits = jnp.where(live[None, :], logits, neg_large)
            top = jnp.max(logits, axis=1, keepdims=True)
            total = jnp.sum(jnp.where(live[None, :], jnp.exp(logits - top), 0.0), axis=1, keepdims=True)
            log_norm = top + jnp.log(total)
            weights = jnp.where(live[None, :], jnp.exp(logits - log_norm), 0.0)
            weights_low = weights.astype(jnp.bfloat16)
            outputs = jnp.dot(weights_low, v_head, preferred_element_type=jnp.float32)
            row_delta = jnp.sum(g_part.astype(jnp.float32) * outputs, axis=1, keepdims=True)
            grad_weights = jnp.dot(g_part, v_head.T, preferred_element_type=jnp.float32)
            grad_logits = (0.125 * weights * (grad_weights - row_delta)).astype(jnp.bfloat16)
            dq_part = jnp.dot(grad_logits, k_head, preferred_element_type=jnp.float32)
            dk_acc = dk_acc + jnp.dot(grad_logits.T, q_part, preferred_element_type=jnp.float32)
            dv_acc = dv_acc + jnp.dot(weights_low.T, g_part, preferred_element_type=jnp.float32)
            return (dk_acc, dv_acc), dq_part

        zeros = jnp.zeros((TOKENS, HD), jnp.float32)
        (dk_all, dv_all), dq_all = lax.scan(one, (zeros, zeros), jnp.arange(count, dtype=jnp.int32))
        return dq_all.reshape(TOKENS, HD), dk_all, dv_all

    dq, dk, dv = lax.map(per_head, jnp.arange(HEADS, dtype=jnp.int32))

    def arrange(grads):
        return jnp.transpose(grads, (1, 0, 2)).reshape(TOKENS, HEADS * HD).astype(jnp.float32)

    return (arrange(dq), arrange(dk), arrange(dv))
```

```python
import functools

import jax
import jax.numpy as jnp
from jax import lax
from jax.experimental import pallas as pl
from jax.experimental.pallas import tpu as pltpu
from jax.sharding import PartitionSpec as P

HD = 64
FRAME = 32


scale_factor = 0.125
neg_large = -1e30


def shifted(x, axis, by):
    peers = lax.axis_size(axis)
    return lax.ppermute(x, axis, [(i, (i + by) % peers) for i in range(peers)])


def token_meta(start, count, valid, views):
    token_ids = start + jnp.arange(count, dtype=jnp.int32)
    frame_ids = token_ids // FRAME
    onehot = frame_ids[:, None] == jnp.arange(valid.shape[0], dtype=jnp.int32)[None, :]
    limits = jnp.sum(jnp.where(onehot, valid[None, :], 0), axis=1)
    labels = jnp.sum(jnp.where(onehot, views[None, :], 0), axis=1)
    return (token_ids % FRAME < limits, labels)


def split_heads(matrix, head_count):
    return matrix.reshape(matrix.shape[0], head_count, matrix.shape[1] // head_count)


def make_logits(q_part, k_part, q_label, k_live, k_label, bias):
    head_count = bias.shape[0]
    raw = jnp.einsum(
        "ihd,jhd->hij",
        split_heads(q_part, head_count),
        split_heads(k_part, head_count),
        preferred_element_type=jnp.float32,
    )
    cross = (q_label[:, None] != k_label[None, :]).astype(jnp.float32)
    raw = raw * scale_factor + bias[:, None, None] * cross[None]
    return jnp.where(k_live[None, None, :], raw, neg_large)


def block_grads(
    q_part, g_part, log_norm, row_delta, k_part, v_part, q_label, k_live, k_label, bias
):
    head_count = bias.shape[0]
    logits = make_logits(q_part, k_part, q_label, k_live, k_label, bias)
    weights = jnp.where(k_live[None, None, :], jnp.exp(logits - log_norm[:, :, None]), 0.0)
    weights_low = weights.astype(jnp.bfloat16)
    g_heads = split_heads(g_part, head_count)
    grad_v = jnp.einsum("hij,ihd->jhd", weights_low, g_heads, preferred_element_type=jnp.float32)
    grad_weights = jnp.einsum(
        "ihd,jhd->hij", g_heads, split_heads(v_part, head_count), preferred_element_type=jnp.float32
    )
    grad_logits = (scale_factor * weights * (grad_weights - row_delta[:, :, None])).astype(
        jnp.bfloat16
    )
    grad_q = jnp.einsum(
        "hij,jhd->ihd",
        grad_logits,
        split_heads(k_part, head_count),
        preferred_element_type=jnp.float32,
    )
    grad_k = jnp.einsum(
        "hij,ihd->jhd",
        grad_logits,
        split_heads(q_part, head_count),
        preferred_element_type=jnp.float32,
    )
    return (
        grad_q.reshape(q_part.shape[0], -1),
        grad_k.reshape(k_part.shape[0], -1),
        grad_v.reshape(k_part.shape[0], -1),
    )


def local_general(query, keys, values, grad_out, valid, views, cross_bias):
    q_local, k_local, v_local, g_local = (
        lax.all_to_all(query, "head", split_axis=1, concat_axis=0, tiled=True),
        lax.all_to_all(keys, "head", split_axis=1, concat_axis=0, tiled=True),
        lax.all_to_all(values, "head", split_axis=1, concat_axis=0, tiled=True),
        lax.all_to_all(grad_out, "head", split_axis=1, concat_axis=0, tiled=True),
    )
    row_count = q_local.shape[0]
    feat_width = q_local.shape[1]
    head_count = feat_width // HD
    cycle_size = lax.axis_size("blk")
    cycle_pos = lax.axis_index("blk")
    head_pos = lax.axis_index("head")
    bias_here = lax.dynamic_slice_in_dim(cross_bias, head_pos * head_count, head_count)
    own_start = cycle_pos * row_count
    own_live, own_label = token_meta(own_start, row_count, valid, views)
    init = (
        jnp.full((head_count, row_count), neg_large, jnp.float32),
        jnp.zeros((head_count, row_count), jnp.float32),
        jnp.zeros((head_count, row_count, HD), jnp.float32),
    )
    zeros = jnp.zeros((row_count, feat_width), jnp.float32)
    carry = init
    k_piece = lax.all_gather(k_local, "blk", axis=0, tiled=True)
    v_piece = lax.all_gather(v_local, "blk", axis=0, tiled=True)
    piece_len = k_piece.shape[0]
    k_blocks = k_piece.reshape(piece_len // row_count, row_count, feat_width)
    v_blocks = v_piece.reshape(piece_len // row_count, row_count, feat_width)

    def one_block(state, item):
        k_block, v_block, index = item
        live, label = token_meta(index * row_count, row_count, valid, views)
        logits = make_logits(q_local, k_block, own_label, live, label, bias_here)
        top_old, total_old, sums_old = state
        top_new = jnp.maximum(top_old, jnp.max(logits, axis=2))
        expo_vals = jnp.where(live[None, None, :], jnp.exp(logits - top_new[:, :, None]), 0.0)
        factor = jnp.exp(top_old - top_new)
        total_new = total_old * factor + jnp.sum(expo_vals, axis=2)
        added = jnp.einsum(
            "hij,jhd->hid",
            expo_vals.astype(jnp.bfloat16),
            split_heads(v_block, head_count),
            preferred_element_type=jnp.float32,
        )
        return ((top_new, total_new, sums_old * factor[:, :, None] + added), None)

    carry, _ = lax.scan(
        one_block, carry, (k_blocks, v_blocks, jnp.arange(piece_len // row_count, dtype=jnp.int32))
    )
    top_all, total_all, sums_all = carry
    norm_rows = top_all + jnp.log(total_all)
    outputs = sums_all / total_all[:, :, None]
    delta_rows = jnp.einsum(
        "ihd,hid->hi", split_heads(g_local, head_count).astype(jnp.float32), outputs
    )

    def key_step(turn, state):
        k_cur, v_cur, dk_cur, dv_cur, dq_cur = state
        anchor = (cycle_pos - turn) % cycle_size
        live, label = token_meta(anchor * row_count, row_count, valid, views)
        dq_add, dk_add, dv_add = block_grads(
            q_local, g_local, norm_rows, delta_rows, k_cur, v_cur, own_label, live, label, bias_here
        )
        k_next, v_next = shifted((k_cur, v_cur), "blk", 1)
        dk_next, dv_next = shifted((dk_cur + dk_add, dv_cur + dv_add), "blk", 1)
        return (k_next, v_next, dk_next, dv_next, dq_cur + dq_add)

    final = lax.fori_loop(0, cycle_size, key_step, (k_local, v_local, zeros, zeros, zeros))
    dq_total, dk_total, dv_total = (final[4], final[2], final[3])
    grads_back = (dq_total, dk_total, dv_total)
    grad_query, grad_keys, grad_values = (
        lax.all_to_all(grads_back[0], "head", split_axis=0, concat_axis=1, tiled=True),
        lax.all_to_all(grads_back[1], "head", split_axis=0, concat_axis=1, tiled=True),
        lax.all_to_all(grads_back[2], "head", split_axis=0, concat_axis=1, tiled=True),
    )
    return (grad_query, grad_keys, grad_values)


MESH = pl.DeviceIdType.MESH


def fused_kernel(
    n_head,
    pairs,
    tok,
    q_hbm,
    k_hbm,
    v_hbm,
    g_hbm,
    valid_hbm,
    views_hbm,
    bias_hbm,
    out_ref,
    q_ref,
    k_ref,
    v_ref,
    g_ref,
    valid_ref,
    views_ref,
    bias_ref,
    in_sem,
    up_sem,
    down_sem,
    sendbuf,
    rbuf,
    obuf,
    w_scr,
    kv_scr,
    kt_scr,
    t_scr,
    ps_scr,
    xsend,
    xrecv,
    own_kv,
    retbuf,
    send_sem,
    recv_sem,
    fsend_sem,
    frecv_sem,
    xsend_sem,
    xrecv_sem,
    rsend_sem,
    rrecv_sem,
):
    fpd = tok // FRAME
    half = pairs * tok
    per_row = n_head // 2
    hpos = lax.axis_index("head")
    me = lax.axis_index("blk") * n_head + hpos
    pair = me // 2
    core = me % 2

    def device(which_pair, which_core):
        return {
            "blk": which_pair // per_row,
            "head": (which_pair % per_row) * 2 + which_core,
        }

    sibling = device(pair, 1 - core)

    def partner(step):
        other, bit = 0, 1
        while bit < pairs:
            other = other + (pair // bit + step // bit) % 2 * bit
            bit *= 2
        return other


    sources = (q_hbm, k_hbm, v_hbm, g_hbm, valid_hbm, views_hbm, bias_hbm)
    targets = (q_ref, k_ref, v_ref, g_ref, valid_ref, views_ref, bias_ref)
    loads = [
        pltpu.make_async_copy(source, target, in_sem.at[i])
        for i, (source, target) in enumerate(zip(sources, targets))
    ]
    for load in loads:
        load.start()

    n_blk = pairs // per_row
    row_pos = pair // per_row
    across = pair + 1 - 2 * (pair % 2)

    def greet(semaphore, which_pair):
        pl.semaphore_signal(
            semaphore, inc=1, device_id=device(which_pair, core), device_id_type=MESH
        )

    barrier = pltpu.get_barrier_semaphore()
    greet(barrier, across)

    @pl.when(row_pos + 1 < n_blk)
    def _():
        greet(barrier, pair + per_row)

    @pl.when(row_pos > 0)
    def _():
        greet(barrier, pair - per_row)

    pl.semaphore_signal(barrier, inc=1, device_id=sibling, device_id_type=MESH)

    for load in loads:
        load.wait()

    for j in range(pairs // 2):
        cols = slice(j * 2 * HD, (j + 1) * 2 * HD)
        qq = q_ref[:, cols] * jnp.bfloat16(scale_factor)
        kk = k_ref[:, cols]
        vv = v_ref[:, cols]
        gg = g_ref[:, cols]
        sendbuf[2 * j, 0:tok, :] = jnp.concatenate([kk[:, :HD], vv[:, :HD]], axis=1)
        sendbuf[2 * j, tok:, :] = jnp.concatenate([qq[:, :HD], gg[:, :HD]], axis=1)
        sendbuf[2 * j + 1, 0:tok, :] = jnp.concatenate([kk[:, HD:], vv[:, HD:]], axis=1)
        sendbuf[2 * j + 1, tok:, :] = jnp.concatenate([qq[:, HD:], gg[:, HD:]], axis=1)

    heard = 2 + (row_pos + n_blk - 1) // n_blk + (2 * n_blk - 2 - row_pos) // n_blk
    pl.semaphore_wait(barrier, heard)

    def out_copy(to):
        return pltpu.make_async_remote_copy(
            src_ref=sendbuf.at[to],
            dst_ref=rbuf.at[pair],
            send_sem=send_sem.at[to],
            recv_sem=recv_sem.at[pair],
            device_id=device(to, core),
            device_id_type=MESH,
        )

    def in_copy(source):
        return pltpu.make_async_remote_copy(
            src_ref=sendbuf.at[source],
            dst_ref=rbuf.at[source],
            send_sem=send_sem.at[source],
            recv_sem=recv_sem.at[source],
            device_id=device(source, core),
            device_id_type=MESH,
        )

    def forward(source):
        return pltpu.make_async_remote_copy(
            src_ref=rbuf.at[source, pl.ds(0, tok)],
            dst_ref=obuf.at[source],
            send_sem=fsend_sem.at[source],
            recv_sem=frecv_sem.at[source],
            device_id=sibling,
            device_id_type=MESH,
        )

    def send_rows(base, distance):
        @pl.when(row_pos + distance < n_blk)
        def _():
            out_copy(base + distance * per_row).start()

        @pl.when(row_pos >= distance)
        def _():
            out_copy(base - distance * per_row).start()

    def pass_word(turn):
        @pl.when(row_pos + 1 < n_blk)
        def _():
            greet(up_sem.at[turn - 1], pair + per_row)

        @pl.when(row_pos > 0)
        def _():
            greet(down_sem.at[turn - 1], pair - per_row)

    def hear_word(turn):
        @pl.when(row_pos > 0)
        def _():
            pl.semaphore_wait(up_sem.at[turn - 1], 1)

        @pl.when(row_pos + 1 < n_blk)
        def _():
            pl.semaphore_wait(down_sem.at[turn - 1], 1)

    pass_word(1)
    send_rows(pair, 1)
    out_copy(across).start()
    rbuf[pair] = sendbuf[pair]
    forward(pair).start()
    for turn in range(1, n_blk):
        hear_word(turn)
        if turn + 1 < n_blk:
            pass_word(turn + 1)
        send_rows(across, turn)
        if turn + 1 < n_blk:
            send_rows(pair, turn + 1)

    bias = bias_ref[pair]
    lanes = per_row * tok
    both = 2 * lanes
    lane = lax.broadcasted_iota(jnp.int32, (8, lanes), 1)
    low = lax.broadcasted_iota(jnp.int32, (lanes, 2 * HD), 1) < HD
    row = lax.broadcasted_iota(jnp.int32, (FRAME, lanes), 0)
    chunks = lanes // FRAME

    def row_at(k):
        upper = row_pos // (n_blk // 2)
        if k < n_blk // 2:
            other, bit = 0, 1
            while bit < n_blk:
                other = other + (row_pos // bit + k // bit) % 2 * bit
                bit *= 2
            return other
        return k + upper * (n_blk - 1 - 2 * k)

    rows_at = [row_at(k) for k in range(n_blk)]

    def signs(k):
        sign_row = jnp.zeros((8, lanes), jnp.float32)
        for c in range(chunks):
            frame = ((rows_at[k] * per_row + c // fpd) * 2 + core) * fpd + c % fpd
            label = views_ref[frame].astype(jnp.float32)
            sign_row = jnp.where(lane // FRAME == c, bias - 2.0 * bias * label, sign_row)
        return sign_row[0:1]

    sign_rows = [signs(k) for k in range(n_blk)]

    def fold(x, op):
        return op(x.reshape(FRAME // 8, 8, lanes), axis=0)

    def low_half(j):
        return slice(j * both, j * both + lanes)

    def high_half(j):
        return slice(j * both + lanes, (j + 1) * both)

    def start_of(part, k):
        return part * half + k * lanes

    def chunk_at(part, k, c):
        return pl.ds(pl.multiple_of(start_of(part, k) + c * FRAME, FRAME), FRAME)

    def over_keys(key_blocks, body, state):
        for part, k in key_blocks:
            owner = core if part == 0 else 1 - core

            def step(c, carry):
                frame = ((rows_at[k] * per_row + c // fpd) * 2 + owner) * fpd + c % fpd
                return body(chunk_at(part, k, c), frame, carry)

            state = lax.fori_loop(0, chunks, step, state, unroll=chunks)
        return state

    def group(key_blocks, query_blocks):
        def mask(at, frame, best):
            view = views_ref[frame].astype(jnp.float32)
            live = row < valid_ref[frame]
            out = []
            for j, b in zip(query_blocks, best):
                x = jnp.where(live, t_scr[at, low_half(j)] + sign_rows[j] * view, neg_large)
                t_scr[at, low_half(j)] = x
                out.append(jnp.maximum(b, fold(x, jnp.max)))
            return tuple(out)

        start = jnp.full((8, lanes), neg_large, jnp.float32)
        tops = over_keys(key_blocks, mask, (start,) * len(query_blocks))
        tops = [jnp.max(t, axis=0, keepdims=True) for t in tops]

        def expo(at, frame, state):
            out = []
            for j, top, (total, delta) in zip(query_blocks, tops, state):
                e = jnp.exp(t_scr[at, low_half(j)] - top)
                t_scr[at, low_half(j)] = e
                out.append(
                    (total + fold(e, jnp.sum), delta + fold(e * t_scr[at, high_half(j)], jnp.sum))
                )
            return tuple(out)

        none = jnp.zeros((8, lanes), jnp.float32)
        sums = over_keys(key_blocks, expo, ((none, none),) * len(query_blocks))
        return [
            (top, jnp.sum(t, axis=0, keepdims=True), jnp.sum(d, axis=0, keepdims=True))
            for top, (t, d) in zip(tops, sums)
        ]

    def scores(kv, w, parts, cols):
        t = lax.dot_general(kv, w, (((1,), (1,)), ((), ())), preferred_element_type=jnp.float32)
        count = t.shape[0] // len(parts)
        for n, first in enumerate(parts):
            t_scr[first : first + count, cols] = t[n * count : (n + 1) * count]

    found = [[] for _ in range(n_blk)]

    def arrive(k):
        for turn in range(per_row):
            source = rows_at[k] * per_row + (pair + turn) % per_row
            if k + turn > 0:
                in_copy(source).wait_recv()
                forward(source).start()

    def keep_keys(part, k, kv):
        kv = kv.reshape(lanes, 2 * HD)
        first = start_of(part, k)
        kv_scr[first : first + lanes, :] = kv
        kt_scr[:, first : first + lanes] = jnp.transpose(kv)[:HD]
        scores(kv, w_scr[0 : (k + 1) * both, :], [first], slice(0, (k + 1) * both))
        for j, stats in enumerate(group([(part, k)], range(k + 1))):
            found[j].append(([(part, k)], stats))

    def stage_own(k):
        base = pl.ds(rows_at[k] * per_row, per_row)
        qg = rbuf[base, tok:, :].reshape(lanes, 2 * HD)
        zero = jnp.zeros_like(qg)
        w_scr[k * both : k * both + lanes, :] = jnp.where(low, qg, zero)
        w_scr[k * both + lanes : (k + 1) * both, :] = jnp.where(low, zero, qg)
        if k > 0:
            w_new = w_scr[k * both : (k + 1) * both, :]
            for part in range(2):
                first = start_of(part, 0)
                old = kv_scr[first : first + k * lanes, :]
                scores(old, w_new, [first], slice(k * both, (k + 1) * both))
            keys = [(part, i) for part in range(2) for i in range(k)]
            found[k].append((keys, group(keys, [k])[0]))
        keep_keys(0, k, rbuf[base, 0:tok, :])

    def stage_other(k):
        for turn in range(per_row):
            forward(rows_at[k] * per_row + turn).wait_recv()
        keep_keys(1, k, obuf[pl.ds(rows_at[k] * per_row, per_row)])

    arrive(0)
    for k in range(n_blk):
        stage_own(k)
        if k + 1 < n_blk:
            arrive(k + 1)
        stage_other(k)

    scales = {}
    deltas = []
    for j in range(n_blk):
        top = functools.reduce(jnp.maximum, [s[0] for _, s in found[j]])
        ratios = [jnp.exp(s[0] - top) for _, s in found[j]]
        inverse = 1.0 / sum(r * s[1] for r, (_, s) in zip(ratios, found[j]))
        deltas.append(sum(r * s[2] for r, (_, s) in zip(ratios, found[j])) * inverse)
        for r, (keys, _) in zip(ratios, found[j]):
            for key in keys:
                scales[key, j] = r * inverse

    pieces = [range(n_blk // 2, n_blk), range(n_blk // 2)]
    wide = n_blk // 2 * lanes

    def kv_grads(part, piece):
        for k in piece:

            def grads(c, carry):
                at = chunk_at(part, k, c)
                for j in range(n_blk):
                    w = t_scr[at, low_half(j)] * scales[(part, k), j]
                    ps_scr[at, high_half(j)] = w.astype(jnp.bfloat16)
                    ds = w * (t_scr[at, high_half(j)] - deltas[j])
                    ps_scr[at, low_half(j)] = ds.astype(jnp.bfloat16)
                return carry

            lax.fori_loop(0, chunks, grads, 0, unroll=chunks)
        first = start_of(part, piece[0])
        return jnp.dot(
            ps_scr[first : first + wide, :], w_scr[...], preferred_element_type=jnp.float32
        )

    def exchange(n):
        at = pl.ds(n * wide, wide)
        return pltpu.make_async_remote_copy(
            src_ref=xsend.at[at],
            dst_ref=xrecv.at[at],
            send_sem=xsend_sem.at[n],
            recv_sem=xrecv_sem.at[n],
            device_id=sibling,
            device_id_type=MESH,
        )

    for n, piece in enumerate(pieces):
        xsend[n * wide : (n + 1) * wide] = kv_grads(1, piece).astype(jnp.bfloat16)
        exchange(n).start()
    for n, piece in enumerate(pieces):
        own_kv[n * wide : (n + 1) * wide] = kv_grads(0, piece)

    def join(n, piece):
        for k in piece:
            dq = jnp.dot(kt_scr[...], ps_scr[:, low_half(k)], preferred_element_type=jnp.float32)
            dq = jnp.transpose(dq * scale_factor).reshape(per_row, tok, HD)
            packed = jnp.concatenate([dq[:, : tok // 2], dq[:, tok // 2 :]], axis=2)
            retbuf[pl.ds(rows_at[k] * per_row, per_row), tok:, :] = packed.astype(jnp.bfloat16)
        exchange(n).wait_recv()
        at = slice(n * wide, (n + 1) * wide)
        dkv = (own_kv[at, :] + xrecv[at, :].astype(jnp.float32)).astype(jnp.bfloat16)
        for i, k in enumerate(piece):
            rows = dkv[i * lanes : (i + 1) * lanes].reshape(per_row, tok, 2 * HD)
            retbuf[pl.ds(rows_at[k] * per_row, per_row), 0:tok, :] = rows
        for k in reversed(piece):
            for turn in range(per_row):
                to = rows_at[k] * per_row + turn
                if k > 0:
                    back(to, pair).start()
                else:

                    @pl.when(to != pair)
                    def _():
                        back(to, pair).start()

    def back(to, slot):
        return pltpu.make_async_remote_copy(
            src_ref=retbuf.at[to],
            dst_ref=out_ref.at[slot],
            send_sem=rsend_sem.at[to],
            recv_sem=rrecv_sem.at[slot],
            device_id=device(to, core),
            device_id_type=MESH,
        )

    for n, piece in enumerate(pieces):
        join(n, piece)
    out_ref[pair] = retbuf[pair]

    for step in range(1, pairs):
        out_copy((pair + step) % pairs).wait_send()
    for step in range(pairs):
        forward((pair + pairs - step) % pairs).wait_send()
    for n in range(2):
        exchange(n).wait_send()
    for step in range(1, pairs):
        source = (pair + pairs - step) % pairs
        back(source, source).wait_recv()
    for step in range(1, pairs):
        back((pair + step) % pairs, pair).wait_send()


def unpack_kernel(pairs, tok, in_ref, dq_ref, dk_ref, dv_ref):
    for j in range(pairs // 2):
        cols = slice(j * 2 * HD, (j + 1) * 2 * HD)
        a = in_ref[2 * j].astype(jnp.float32)
        b = in_ref[2 * j + 1].astype(jnp.float32)
        dk_ref[:, cols] = jnp.concatenate([a[:tok, :HD], b[:tok, :HD]], axis=1)
        dv_ref[:, cols] = jnp.concatenate([a[:tok, HD:], b[:tok, HD:]], axis=1)
        mid = tok // 2
        dq_ref[:mid, cols] = jnp.concatenate([a[tok:, :HD], b[tok:, :HD]], axis=1)
        dq_ref[mid:, cols] = jnp.concatenate([a[tok:, HD:], b[tok:, HD:]], axis=1)


def local_fused(n_head, pairs, *args):
    query, _, _, _, valid, _, cross_bias = args
    tok, width = query.shape
    half = pairs * tok
    vmem = pl.BlockSpec(memory_space=pltpu.VMEM)
    hbm = pl.BlockSpec(memory_space=pltpu.HBM)
    frames = valid.shape[0]
    rows = tok + tok // 2
    dma = pltpu.SemaphoreType.DMA
    packed = pl.pallas_call(
        functools.partial(fused_kernel, n_head, pairs, tok),
        out_shape=jax.ShapeDtypeStruct((pairs, rows, 2 * HD), jnp.bfloat16),
        in_specs=[hbm] * 7,
        out_specs=vmem,
        scratch_shapes=[
            pltpu.VMEM((tok, width), jnp.bfloat16),
            pltpu.VMEM((tok, width), jnp.bfloat16),
            pltpu.VMEM((tok, width), jnp.bfloat16),
            pltpu.VMEM((tok, width), jnp.bfloat16),
            pltpu.SMEM((frames,), jnp.int32),
            pltpu.SMEM((frames,), jnp.int32),
            pltpu.SMEM((cross_bias.shape[0],), jnp.float32),
            dma((7,)),
            pltpu.SemaphoreType.REGULAR((pairs * 2 // n_head - 1,)),
            pltpu.SemaphoreType.REGULAR((pairs * 2 // n_head - 1,)),
            pltpu.VMEM((pairs, 2 * tok, 2 * HD), jnp.bfloat16),
            pltpu.VMEM((pairs, 2 * tok, 2 * HD), jnp.bfloat16),
            pltpu.VMEM((pairs, tok, 2 * HD), jnp.bfloat16),
            pltpu.VMEM((2 * half, 2 * HD), jnp.bfloat16),
            pltpu.VMEM((2 * half, 2 * HD), jnp.bfloat16),
            pltpu.VMEM((HD, 2 * half), jnp.bfloat16),
            pltpu.VMEM((2 * half, 2 * half), jnp.float32),
            pltpu.VMEM((2 * half, 2 * half), jnp.bfloat16),
            pltpu.VMEM((half, 2 * HD), jnp.bfloat16),
            pltpu.VMEM((half, 2 * HD), jnp.bfloat16),
            pltpu.VMEM((half, 2 * HD), jnp.float32),
            pltpu.VMEM((pairs, rows, 2 * HD), jnp.bfloat16),
            dma((pairs,)),
            dma((pairs,)),
            dma((pairs,)),
            dma((pairs,)),
            dma((2,)),
            dma((2,)),
            dma((pairs,)),
            dma((pairs,)),
        ],
        compiler_params=pltpu.CompilerParams(
            collective_id=0, has_side_effects=True, vmem_limit_bytes=24 * 1024 * 1024
        ),
    )(*[pltpu.with_memory_space_constraint(x, pltpu.HBM) for x in args])
    grad = jax.ShapeDtypeStruct((tok, width), jnp.float32)
    return pl.pallas_call(
        functools.partial(unpack_kernel, pairs, tok),
        out_shape=(grad, grad, grad),
        in_specs=[vmem],
        out_specs=(vmem, vmem, vmem),
        compiler_params=pltpu.CompilerParams(vmem_limit_bytes=4 * 1024 * 1024),
    )(packed)


def solution(mesh):
    rows = P(("grp", "blk", "head"), None)
    n_blk, n_head = mesh.shape["blk"], mesh.shape["head"]

    def local(query, keys, values, grad_out, valid, views, cross_bias):
        args = (query, keys, values, grad_out, valid, views, cross_bias)
        tok, width = query.shape
        pairs = n_blk * n_head // 2
        one_each = n_head == 4 and pairs & (pairs - 1) == 0 and pairs * HD == width and cross_bias.shape[0] == pairs
        if one_each and tok % (2 * FRAME) == 0 and tok * pairs <= 1024:
            return local_fused(n_head, pairs, *args)
        return local_general(*args)

    return jax.shard_map(
        local,
        mesh=mesh,
        in_specs=(rows, rows, rows, rows, P("grp"), P("grp"), P()),
        out_specs=(rows, rows, rows),
        check_vma=False,
    )
```

```python
import functools

import jax
import jax.numpy as jnp
from jax import lax
from jax.experimental import pallas as pl
from jax.experimental.pallas import tpu as pltpu
from jax.sharding import PartitionSpec as P

HD = 64
FRAME = 32


scale_factor = 0.125
neg_large = -1e30


def shifted(x, axis, by):
    peers = lax.axis_size(axis)
    return lax.ppermute(x, axis, [(i, (i + by) % peers) for i in range(peers)])


def token_meta(start, count, valid, views):
    token_ids = start + jnp.arange(count, dtype=jnp.int32)
    frame_ids = token_ids // FRAME
    onehot = frame_ids[:, None] == jnp.arange(valid.shape[0], dtype=jnp.int32)[None, :]
    limits = jnp.sum(jnp.where(onehot, valid[None, :], 0), axis=1)
    labels = jnp.sum(jnp.where(onehot, views[None, :], 0), axis=1)
    return (token_ids % FRAME < limits, labels)


def split_heads(matrix, head_count):
    return matrix.reshape(matrix.shape[0], head_count, matrix.shape[1] // head_count)


def make_logits(q_part, k_part, q_label, k_live, k_label, bias):
    head_count = bias.shape[0]
    raw = jnp.einsum(
        "ihd,jhd->hij",
        split_heads(q_part, head_count),
        split_heads(k_part, head_count),
        preferred_element_type=jnp.float32,
    )
    cross = (q_label[:, None] != k_label[None, :]).astype(jnp.float32)
    raw = raw * scale_factor + bias[:, None, None] * cross[None]
    return jnp.where(k_live[None, None, :], raw, neg_large)


def block_grads(
    q_part, g_part, log_norm, row_delta, k_part, v_part, q_label, k_live, k_label, bias
):
    head_count = bias.shape[0]
    logits = make_logits(q_part, k_part, q_label, k_live, k_label, bias)
    weights = jnp.where(k_live[None, None, :], jnp.exp(logits - log_norm[:, :, None]), 0.0)
    weights_low = weights.astype(jnp.bfloat16)
    g_heads = split_heads(g_part, head_count)
    grad_v = jnp.einsum("hij,ihd->jhd", weights_low, g_heads, preferred_element_type=jnp.float32)
    grad_weights = jnp.einsum(
        "ihd,jhd->hij", g_heads, split_heads(v_part, head_count), preferred_element_type=jnp.float32
    )
    grad_logits = (scale_factor * weights * (grad_weights - row_delta[:, :, None])).astype(
        jnp.bfloat16
    )
    grad_q = jnp.einsum(
        "hij,jhd->ihd",
        grad_logits,
        split_heads(k_part, head_count),
        preferred_element_type=jnp.float32,
    )
    grad_k = jnp.einsum(
        "hij,ihd->jhd",
        grad_logits,
        split_heads(q_part, head_count),
        preferred_element_type=jnp.float32,
    )
    return (
        grad_q.reshape(q_part.shape[0], -1),
        grad_k.reshape(k_part.shape[0], -1),
        grad_v.reshape(k_part.shape[0], -1),
    )


def local_general(query, keys, values, grad_out, valid, views, cross_bias):
    q_local, k_local, v_local, g_local = (
        lax.all_to_all(query, "head", split_axis=1, concat_axis=0, tiled=True),
        lax.all_to_all(keys, "head", split_axis=1, concat_axis=0, tiled=True),
        lax.all_to_all(values, "head", split_axis=1, concat_axis=0, tiled=True),
        lax.all_to_all(grad_out, "head", split_axis=1, concat_axis=0, tiled=True),
    )
    row_count = q_local.shape[0]
    feat_width = q_local.shape[1]
    head_count = feat_width // HD
    cycle_size = lax.axis_size("blk")
    cycle_pos = lax.axis_index("blk")
    head_pos = lax.axis_index("head")
    bias_here = lax.dynamic_slice_in_dim(cross_bias, head_pos * head_count, head_count)
    own_start = cycle_pos * row_count
    own_live, own_label = token_meta(own_start, row_count, valid, views)
    init = (
        jnp.full((head_count, row_count), neg_large, jnp.float32),
        jnp.zeros((head_count, row_count), jnp.float32),
        jnp.zeros((head_count, row_count, HD), jnp.float32),
    )
    zeros = jnp.zeros((row_count, feat_width), jnp.float32)
    carry = init
    k_piece = lax.all_gather(k_local, "blk", axis=0, tiled=True)
    v_piece = lax.all_gather(v_local, "blk", axis=0, tiled=True)
    piece_len = k_piece.shape[0]
    k_blocks = k_piece.reshape(piece_len // row_count, row_count, feat_width)
    v_blocks = v_piece.reshape(piece_len // row_count, row_count, feat_width)

    def one_block(state, item):
        k_block, v_block, index = item
        live, label = token_meta(index * row_count, row_count, valid, views)
        logits = make_logits(q_local, k_block, own_label, live, label, bias_here)
        top_old, total_old, sums_old = state
        top_new = jnp.maximum(top_old, jnp.max(logits, axis=2))
        expo_vals = jnp.where(live[None, None, :], jnp.exp(logits - top_new[:, :, None]), 0.0)
        factor = jnp.exp(top_old - top_new)
        total_new = total_old * factor + jnp.sum(expo_vals, axis=2)
        added = jnp.einsum(
            "hij,jhd->hid",
            expo_vals.astype(jnp.bfloat16),
            split_heads(v_block, head_count),
            preferred_element_type=jnp.float32,
        )
        return ((top_new, total_new, sums_old * factor[:, :, None] + added), None)

    carry, _ = lax.scan(
        one_block, carry, (k_blocks, v_blocks, jnp.arange(piece_len // row_count, dtype=jnp.int32))
    )
    top_all, total_all, sums_all = carry
    norm_rows = top_all + jnp.log(total_all)
    outputs = sums_all / total_all[:, :, None]
    delta_rows = jnp.einsum(
        "ihd,hid->hi", split_heads(g_local, head_count).astype(jnp.float32), outputs
    )

    def key_step(turn, state):
        k_cur, v_cur, dk_cur, dv_cur, dq_cur = state
        anchor = (cycle_pos - turn) % cycle_size
        live, label = token_meta(anchor * row_count, row_count, valid, views)
        dq_add, dk_add, dv_add = block_grads(
            q_local, g_local, norm_rows, delta_rows, k_cur, v_cur, own_label, live, label, bias_here
        )
        k_next, v_next = shifted((k_cur, v_cur), "blk", 1)
        dk_next, dv_next = shifted((dk_cur + dk_add, dv_cur + dv_add), "blk", 1)
        return (k_next, v_next, dk_next, dv_next, dq_cur + dq_add)

    final = lax.fori_loop(0, cycle_size, key_step, (k_local, v_local, zeros, zeros, zeros))
    dq_total, dk_total, dv_total = (final[4], final[2], final[3])
    grads_back = (dq_total, dk_total, dv_total)
    grad_query, grad_keys, grad_values = (
        lax.all_to_all(grads_back[0], "head", split_axis=0, concat_axis=1, tiled=True),
        lax.all_to_all(grads_back[1], "head", split_axis=0, concat_axis=1, tiled=True),
        lax.all_to_all(grads_back[2], "head", split_axis=0, concat_axis=1, tiled=True),
    )
    return (grad_query, grad_keys, grad_values)


MESH = pl.DeviceIdType.MESH


def fused_kernel(
    n_head,
    pairs,
    tok,
    q_hbm,
    k_hbm,
    v_hbm,
    g_hbm,
    valid_hbm,
    views_hbm,
    bias_hbm,
    out_ref,
    q_ref,
    k_ref,
    v_ref,
    g_ref,
    valid_ref,
    views_ref,
    bias_ref,
    in_sem,
    word_sem,
    sendbuf,
    rbuf,
    obuf,
    w_scr,
    kv_scr,
    kt_scr,
    t_scr,
    ps_scr,
    xsend,
    xrecv,
    own_kv,
    retbuf,
    send_sem,
    recv_sem,
    fsend_sem,
    frecv_sem,
    xsend_sem,
    xrecv_sem,
    rsend_sem,
    rrecv_sem,
):
    fpd = tok // FRAME
    half = pairs * tok
    per_row = n_head // 2
    hpos = lax.axis_index("head")
    me = lax.axis_index("blk") * n_head + hpos
    pair = me // 2
    core = me % 2

    def device(which_pair, which_core):
        return {
            "blk": which_pair // per_row,
            "head": (which_pair % per_row) * 2 + which_core,
        }

    sibling = device(pair, 1 - core)

    def partner(step):
        other, bit = 0, 1
        while bit < pairs:
            other = other + (pair // bit + step // bit) % 2 * bit
            bit *= 2
        return other


    sources = (q_hbm, k_hbm, v_hbm, g_hbm, valid_hbm, views_hbm, bias_hbm)
    targets = (q_ref, k_ref, v_ref, g_ref, valid_ref, views_ref, bias_ref)
    loads = [
        pltpu.make_async_copy(source, target, in_sem.at[i])
        for i, (source, target) in enumerate(zip(sources, targets))
    ]
    for load in loads:
        load.start()

    n_blk = pairs // per_row
    row_pos = pair // per_row
    across = pair + 1 - 2 * (pair % 2)

    def greet(semaphore, which_pair):
        pl.semaphore_signal(
            semaphore, inc=1, device_id=device(which_pair, core), device_id_type=MESH
        )

    barrier = pltpu.get_barrier_semaphore()
    greet(barrier, across)

    @pl.when(row_pos > 0)
    def _():
        greet(barrier, pair - per_row)

    for to in range(per_row, pairs):

        @pl.when(to // per_row > row_pos)
        def _():
            greet(barrier, to)

    pl.semaphore_signal(barrier, inc=1, device_id=sibling, device_id_type=MESH)

    for load in loads:
        load.wait()

    for j in range(pairs // 2):
        cols = slice(j * 2 * HD, (j + 1) * 2 * HD)
        qq = q_ref[:, cols] * jnp.bfloat16(scale_factor)
        kk = k_ref[:, cols]
        vv = v_ref[:, cols]
        gg = g_ref[:, cols]
        sendbuf[2 * j, 0:tok, :] = jnp.concatenate([kk[:, :HD], vv[:, :HD]], axis=1)
        sendbuf[2 * j, tok:, :] = jnp.concatenate([qq[:, :HD], gg[:, :HD]], axis=1)
        sendbuf[2 * j + 1, 0:tok, :] = jnp.concatenate([kk[:, HD:], vv[:, HD:]], axis=1)
        sendbuf[2 * j + 1, tok:, :] = jnp.concatenate([qq[:, HD:], gg[:, HD:]], axis=1)

    heard = 2 + row_pos * per_row + (2 * n_blk - 2 - row_pos) // n_blk
    pl.semaphore_wait(barrier, heard)

    def out_copy(to):
        return pltpu.make_async_remote_copy(
            src_ref=sendbuf.at[to],
            dst_ref=rbuf.at[pair],
            send_sem=send_sem.at[to],
            recv_sem=recv_sem.at[pair],
            device_id=device(to, core),
            device_id_type=MESH,
        )

    def in_copy(source):
        return pltpu.make_async_remote_copy(
            src_ref=sendbuf.at[source],
            dst_ref=rbuf.at[source],
            send_sem=send_sem.at[source],
            recv_sem=recv_sem.at[source],
            device_id=device(source, core),
            device_id_type=MESH,
        )

    def forward(source):
        return pltpu.make_async_remote_copy(
            src_ref=rbuf.at[source, pl.ds(0, tok)],
            dst_ref=obuf.at[source],
            send_sem=fsend_sem.at[source],
            recv_sem=frecv_sem.at[source],
            device_id=sibling,
            device_id_type=MESH,
        )

    def send_up(base, distance):
        @pl.when(row_pos + distance < n_blk)
        def _():
            out_copy(base + distance * per_row).start()

    def pass_word(turn):
        @pl.when(row_pos > 0)
        def _():
            greet(word_sem.at[turn - 1], pair - per_row)

    pass_word(1)
    for to in reversed(range(pairs - per_row)):

        @pl.when(to // per_row < row_pos)
        def _():
            out_copy(to).start()

    send_up(pair, 1)
    out_copy(across).start()
    rbuf[pair] = sendbuf[pair]
    forward(pair).start()
    for turn in range(1, n_blk):

        @pl.when(row_pos + 1 < n_blk)
        def _():
            pl.semaphore_wait(word_sem.at[turn - 1], 1)

        if turn + 1 < n_blk:
            pass_word(turn + 1)
        send_up(across, turn)
        if turn + 1 < n_blk:
            send_up(pair, turn + 1)

    bias = bias_ref[pair]
    lanes = per_row * tok
    both = 2 * lanes
    lane = lax.broadcasted_iota(jnp.int32, (8, lanes), 1)
    low = lax.broadcasted_iota(jnp.int32, (lanes, 2 * HD), 1) < HD
    row = lax.broadcasted_iota(jnp.int32, (FRAME, lanes), 0)
    chunks = lanes // FRAME

    def row_at(k):
        upper = row_pos // (n_blk // 2)
        if k < n_blk // 2:
            other, bit = 0, 1
            while bit < n_blk:
                other = other + (row_pos // bit + k // bit) % 2 * bit
                bit *= 2
            return other
        return k + upper * (n_blk - 1 - 2 * k)

    rows_at = [row_at(k) for k in range(n_blk)]

    def signs(k):
        sign_row = jnp.zeros((8, lanes), jnp.float32)
        for c in range(chunks):
            frame = ((rows_at[k] * per_row + c // fpd) * 2 + core) * fpd + c % fpd
            label = views_ref[frame].astype(jnp.float32)
            sign_row = jnp.where(lane // FRAME == c, bias - 2.0 * bias * label, sign_row)
        return sign_row[0:1]

    sign_rows = [signs(k) for k in range(n_blk)]

    def fold(x, op):
        return op(x.reshape(FRAME // 8, 8, lanes), axis=0)

    def low_half(j):
        return slice(j * both, j * both + lanes)

    def high_half(j):
        return slice(j * both + lanes, (j + 1) * both)

    def start_of(part, k):
        return part * half + k * lanes

    def chunk_at(part, k, c):
        return pl.ds(pl.multiple_of(start_of(part, k) + c * FRAME, FRAME), FRAME)

    def over_keys(key_blocks, body, state):
        for part, k in key_blocks:
            owner = core if part == 0 else 1 - core

            def step(c, carry):
                frame = ((rows_at[k] * per_row + c // fpd) * 2 + owner) * fpd + c % fpd
                return body(chunk_at(part, k, c), frame, carry)

            state = lax.fori_loop(0, chunks, step, state, unroll=chunks)
        return state

    def group(key_blocks, query_blocks):
        def mask(at, frame, best):
            view = views_ref[frame].astype(jnp.float32)
            live = row < valid_ref[frame]
            out = []
            for j, b in zip(query_blocks, best):
                x = jnp.where(live, t_scr[at, low_half(j)] + sign_rows[j] * view, neg_large)
                t_scr[at, low_half(j)] = x
                out.append(jnp.maximum(b, fold(x, jnp.max)))
            return tuple(out)

        start = jnp.full((8, lanes), neg_large, jnp.float32)
        tops = over_keys(key_blocks, mask, (start,) * len(query_blocks))
        tops = [jnp.max(t, axis=0, keepdims=True) for t in tops]

        def expo(at, frame, state):
            out = []
            for j, top, (total, delta) in zip(query_blocks, tops, state):
                e = jnp.exp(t_scr[at, low_half(j)] - top)
                t_scr[at, low_half(j)] = e
                out.append(
                    (total + fold(e, jnp.sum), delta + fold(e * t_scr[at, high_half(j)], jnp.sum))
                )
            return tuple(out)

        none = jnp.zeros((8, lanes), jnp.float32)
        sums = over_keys(key_blocks, expo, ((none, none),) * len(query_blocks))
        return [
            (top, jnp.sum(t, axis=0, keepdims=True), jnp.sum(d, axis=0, keepdims=True))
            for top, (t, d) in zip(tops, sums)
        ]

    def scores(kv, w, parts, cols):
        t = lax.dot_general(kv, w, (((1,), (1,)), ((), ())), preferred_element_type=jnp.float32)
        count = t.shape[0] // len(parts)
        for n, first in enumerate(parts):
            t_scr[first : first + count, cols] = t[n * count : (n + 1) * count]

    found = [[] for _ in range(n_blk)]

    def arrive(k):
        for turn in range(per_row):
            source = rows_at[k] * per_row + (pair + turn) % per_row
            if k + turn > 0:
                in_copy(source).wait_recv()
                forward(source).start()

    def keep_keys(part, k, kv):
        kv = kv.reshape(lanes, 2 * HD)
        first = start_of(part, k)
        kv_scr[first : first + lanes, :] = kv
        kt_scr[:, first : first + lanes] = jnp.transpose(kv)[:HD]
        scores(kv, w_scr[0 : (k + 1) * both, :], [first], slice(0, (k + 1) * both))
        for j, stats in enumerate(group([(part, k)], range(k + 1))):
            found[j].append(([(part, k)], stats))

    def stage_own(k):
        base = pl.ds(rows_at[k] * per_row, per_row)
        qg = rbuf[base, tok:, :].reshape(lanes, 2 * HD)
        zero = jnp.zeros_like(qg)
        w_scr[k * both : k * both + lanes, :] = jnp.where(low, qg, zero)
        w_scr[k * both + lanes : (k + 1) * both, :] = jnp.where(low, zero, qg)
        if k > 0:
            w_new = w_scr[k * both : (k + 1) * both, :]
            for part in range(2):
                first = start_of(part, 0)
                old = kv_scr[first : first + k * lanes, :]
                scores(old, w_new, [first], slice(k * both, (k + 1) * both))
            keys = [(part, i) for part in range(2) for i in range(k)]
            found[k].append((keys, group(keys, [k])[0]))
        keep_keys(0, k, rbuf[base, 0:tok, :])

    def stage_other(k):
        for turn in range(per_row):
            forward(rows_at[k] * per_row + turn).wait_recv()
        keep_keys(1, k, obuf[pl.ds(rows_at[k] * per_row, per_row)])

    arrive(0)
    for k in range(n_blk):
        stage_own(k)
        if k + 1 < n_blk:
            arrive(k + 1)
        stage_other(k)

    scales = {}
    deltas = []
    for j in range(n_blk):
        top = functools.reduce(jnp.maximum, [s[0] for _, s in found[j]])
        ratios = [jnp.exp(s[0] - top) for _, s in found[j]]
        inverse = 1.0 / sum(r * s[1] for r, (_, s) in zip(ratios, found[j]))
        deltas.append(sum(r * s[2] for r, (_, s) in zip(ratios, found[j])) * inverse)
        for r, (keys, _) in zip(ratios, found[j]):
            for key in keys:
                scales[key, j] = r * inverse

    pieces = [range(n_blk // 2, n_blk), range(n_blk // 2)]
    wide = n_blk // 2 * lanes

    def kv_grads(part, piece):
        for k in piece:

            def grads(c, carry):
                at = chunk_at(part, k, c)
                for j in range(n_blk):
                    w = t_scr[at, low_half(j)] * scales[(part, k), j]
                    ps_scr[at, high_half(j)] = w.astype(jnp.bfloat16)
                    ds = w * (t_scr[at, high_half(j)] - deltas[j])
                    ps_scr[at, low_half(j)] = ds.astype(jnp.bfloat16)
                return carry

            lax.fori_loop(0, chunks, grads, 0, unroll=chunks)
        first = start_of(part, piece[0])
        return jnp.dot(
            ps_scr[first : first + wide, :], w_scr[...], preferred_element_type=jnp.float32
        )

    def exchange(n):
        at = pl.ds(n * wide, wide)
        return pltpu.make_async_remote_copy(
            src_ref=xsend.at[at],
            dst_ref=xrecv.at[at],
            send_sem=xsend_sem.at[n],
            recv_sem=xrecv_sem.at[n],
            device_id=sibling,
            device_id_type=MESH,
        )

    for n, piece in enumerate(pieces):
        xsend[n * wide : (n + 1) * wide] = kv_grads(1, piece).astype(jnp.bfloat16)
        exchange(n).start()
    for n, piece in enumerate(pieces):
        own_kv[n * wide : (n + 1) * wide] = kv_grads(0, piece)

    def join(n, piece):
        for k in piece:
            dq = jnp.dot(kt_scr[...], ps_scr[:, low_half(k)], preferred_element_type=jnp.float32)
            dq = jnp.transpose(dq * scale_factor).reshape(per_row, tok, HD)
            packed = jnp.concatenate([dq[:, : tok // 2], dq[:, tok // 2 :]], axis=2)
            retbuf[pl.ds(rows_at[k] * per_row, per_row), tok:, :] = packed.astype(jnp.bfloat16)
        exchange(n).wait_recv()
        at = slice(n * wide, (n + 1) * wide)
        dkv = (own_kv[at, :] + xrecv[at, :].astype(jnp.float32)).astype(jnp.bfloat16)
        for i, k in enumerate(piece):
            rows = dkv[i * lanes : (i + 1) * lanes].reshape(per_row, tok, 2 * HD)
            retbuf[pl.ds(rows_at[k] * per_row, per_row), 0:tok, :] = rows
        for k in reversed(piece):
            for turn in range(per_row):
                to = rows_at[k] * per_row + turn
                if k > 0:
                    back(to, pair).start()
                else:

                    @pl.when(to != pair)
                    def _():
                        back(to, pair).start()

    def back(to, slot):
        return pltpu.make_async_remote_copy(
            src_ref=retbuf.at[to],
            dst_ref=out_ref.at[slot],
            send_sem=rsend_sem.at[to],
            recv_sem=rrecv_sem.at[slot],
            device_id=device(to, core),
            device_id_type=MESH,
        )

    for n, piece in enumerate(pieces):
        join(n, piece)
    out_ref[pair] = retbuf[pair]

    for step in range(1, pairs):
        out_copy((pair + step) % pairs).wait_send()
    for step in range(pairs):
        forward((pair + pairs - step) % pairs).wait_send()
    for n in range(2):
        exchange(n).wait_send()
    for step in range(1, pairs):
        source = (pair + pairs - step) % pairs
        back(source, source).wait_recv()
    for step in range(1, pairs):
        back((pair + step) % pairs, pair).wait_send()


def unpack_kernel(pairs, tok, in_ref, dq_ref, dk_ref, dv_ref):
    for j in range(pairs // 2):
        cols = slice(j * 2 * HD, (j + 1) * 2 * HD)
        a = in_ref[2 * j].astype(jnp.float32)
        b = in_ref[2 * j + 1].astype(jnp.float32)
        dk_ref[:, cols] = jnp.concatenate([a[:tok, :HD], b[:tok, :HD]], axis=1)
        dv_ref[:, cols] = jnp.concatenate([a[:tok, HD:], b[:tok, HD:]], axis=1)
        mid = tok // 2
        dq_ref[:mid, cols] = jnp.concatenate([a[tok:, :HD], b[tok:, :HD]], axis=1)
        dq_ref[mid:, cols] = jnp.concatenate([a[tok:, HD:], b[tok:, HD:]], axis=1)


def local_fused(n_head, pairs, *args):
    query, _, _, _, valid, _, cross_bias = args
    tok, width = query.shape
    half = pairs * tok
    vmem = pl.BlockSpec(memory_space=pltpu.VMEM)
    hbm = pl.BlockSpec(memory_space=pltpu.HBM)
    frames = valid.shape[0]
    rows = tok + tok // 2
    dma = pltpu.SemaphoreType.DMA
    packed = pl.pallas_call(
        functools.partial(fused_kernel, n_head, pairs, tok),
        out_shape=jax.ShapeDtypeStruct((pairs, rows, 2 * HD), jnp.bfloat16),
        in_specs=[hbm] * 7,
        out_specs=vmem,
        scratch_shapes=[
            pltpu.VMEM((tok, width), jnp.bfloat16),
            pltpu.VMEM((tok, width), jnp.bfloat16),
            pltpu.VMEM((tok, width), jnp.bfloat16),
            pltpu.VMEM((tok, width), jnp.bfloat16),
            pltpu.SMEM((frames,), jnp.int32),
            pltpu.SMEM((frames,), jnp.int32),
            pltpu.SMEM((cross_bias.shape[0],), jnp.float32),
            dma((7,)),
            pltpu.SemaphoreType.REGULAR((pairs * 2 // n_head - 1,)),
            pltpu.VMEM((pairs, 2 * tok, 2 * HD), jnp.bfloat16),
            pltpu.VMEM((pairs, 2 * tok, 2 * HD), jnp.bfloat16),
            pltpu.VMEM((pairs, tok, 2 * HD), jnp.bfloat16),
            pltpu.VMEM((2 * half, 2 * HD), jnp.bfloat16),
            pltpu.VMEM((2 * half, 2 * HD), jnp.bfloat16),
            pltpu.VMEM((HD, 2 * half), jnp.bfloat16),
            pltpu.VMEM((2 * half, 2 * half), jnp.float32),
            pltpu.VMEM((2 * half, 2 * half), jnp.bfloat16),
            pltpu.VMEM((half, 2 * HD), jnp.bfloat16),
            pltpu.VMEM((half, 2 * HD), jnp.bfloat16),
            pltpu.VMEM((half, 2 * HD), jnp.float32),
            pltpu.VMEM((pairs, rows, 2 * HD), jnp.bfloat16),
            dma((pairs,)),
            dma((pairs,)),
            dma((pairs,)),
            dma((pairs,)),
            dma((2,)),
            dma((2,)),
            dma((pairs,)),
            dma((pairs,)),
        ],
        compiler_params=pltpu.CompilerParams(
            collective_id=0, has_side_effects=True, vmem_limit_bytes=24 * 1024 * 1024
        ),
    )(*[pltpu.with_memory_space_constraint(x, pltpu.HBM) for x in args])
    grad = jax.ShapeDtypeStruct((tok, width), jnp.float32)
    return pl.pallas_call(
        functools.partial(unpack_kernel, pairs, tok),
        out_shape=(grad, grad, grad),
        in_specs=[vmem],
        out_specs=(vmem, vmem, vmem),
        compiler_params=pltpu.CompilerParams(vmem_limit_bytes=4 * 1024 * 1024),
    )(packed)


def solution(mesh):
    rows = P(("grp", "blk", "head"), None)
    n_blk, n_head = mesh.shape["blk"], mesh.shape["head"]

    def local(query, keys, values, grad_out, valid, views, cross_bias):
        args = (query, keys, values, grad_out, valid, views, cross_bias)
        tok, width = query.shape
        pairs = n_blk * n_head // 2
        one_each = n_head == 4 and pairs & (pairs - 1) == 0 and pairs * HD == width and cross_bias.shape[0] == pairs
        if one_each and tok % (2 * FRAME) == 0 and tok * pairs <= 1024:
            return local_fused(n_head, pairs, *args)
        return local_general(*args)

    return jax.shard_map(
        local,
        mesh=mesh,
        in_specs=(rows, rows, rows, rows, P("grp"), P("grp"), P()),
        out_specs=(rows, rows, rows),
        check_vma=False,
    )
```

```python
import functools

import jax
import jax.numpy as jnp
from jax import lax
from jax.experimental import pallas as pl
from jax.experimental.pallas import tpu as pltpu
from jax.sharding import PartitionSpec as P

HD = 64
FRAME = 32


scale_factor = 0.125
neg_large = -1e30


def shifted(x, axis, by):
    peers = lax.axis_size(axis)
    return lax.ppermute(x, axis, [(i, (i + by) % peers) for i in range(peers)])


def token_meta(start, count, valid, views):
    token_ids = start + jnp.arange(count, dtype=jnp.int32)
    frame_ids = token_ids // FRAME
    onehot = frame_ids[:, None] == jnp.arange(valid.shape[0], dtype=jnp.int32)[None, :]
    limits = jnp.sum(jnp.where(onehot, valid[None, :], 0), axis=1)
    labels = jnp.sum(jnp.where(onehot, views[None, :], 0), axis=1)
    return (token_ids % FRAME < limits, labels)


def split_heads(matrix, head_count):
    return matrix.reshape(matrix.shape[0], head_count, matrix.shape[1] // head_count)


def make_logits(q_part, k_part, q_label, k_live, k_label, bias):
    head_count = bias.shape[0]
    raw = jnp.einsum(
        "ihd,jhd->hij",
        split_heads(q_part, head_count),
        split_heads(k_part, head_count),
        preferred_element_type=jnp.float32,
    )
    cross = (q_label[:, None] != k_label[None, :]).astype(jnp.float32)
    raw = raw * scale_factor + bias[:, None, None] * cross[None]
    return jnp.where(k_live[None, None, :], raw, neg_large)


def block_grads(
    q_part, g_part, log_norm, row_delta, k_part, v_part, q_label, k_live, k_label, bias
):
    head_count = bias.shape[0]
    logits = make_logits(q_part, k_part, q_label, k_live, k_label, bias)
    weights = jnp.where(k_live[None, None, :], jnp.exp(logits - log_norm[:, :, None]), 0.0)
    weights_low = weights.astype(jnp.bfloat16)
    g_heads = split_heads(g_part, head_count)
    grad_v = jnp.einsum("hij,ihd->jhd", weights_low, g_heads, preferred_element_type=jnp.float32)
    grad_weights = jnp.einsum(
        "ihd,jhd->hij", g_heads, split_heads(v_part, head_count), preferred_element_type=jnp.float32
    )
    grad_logits = (scale_factor * weights * (grad_weights - row_delta[:, :, None])).astype(
        jnp.bfloat16
    )
    grad_q = jnp.einsum(
        "hij,jhd->ihd",
        grad_logits,
        split_heads(k_part, head_count),
        preferred_element_type=jnp.float32,
    )
    grad_k = jnp.einsum(
        "hij,ihd->jhd",
        grad_logits,
        split_heads(q_part, head_count),
        preferred_element_type=jnp.float32,
    )
    return (
        grad_q.reshape(q_part.shape[0], -1),
        grad_k.reshape(k_part.shape[0], -1),
        grad_v.reshape(k_part.shape[0], -1),
    )


def local_general(query, keys, values, grad_out, valid, views, cross_bias):
    q_local, k_local, v_local, g_local = (
        lax.all_to_all(query, "head", split_axis=1, concat_axis=0, tiled=True),
        lax.all_to_all(keys, "head", split_axis=1, concat_axis=0, tiled=True),
        lax.all_to_all(values, "head", split_axis=1, concat_axis=0, tiled=True),
        lax.all_to_all(grad_out, "head", split_axis=1, concat_axis=0, tiled=True),
    )
    row_count = q_local.shape[0]
    feat_width = q_local.shape[1]
    head_count = feat_width // HD
    cycle_size = lax.axis_size("blk")
    cycle_pos = lax.axis_index("blk")
    head_pos = lax.axis_index("head")
    bias_here = lax.dynamic_slice_in_dim(cross_bias, head_pos * head_count, head_count)
    own_start = cycle_pos * row_count
    own_live, own_label = token_meta(own_start, row_count, valid, views)
    init = (
        jnp.full((head_count, row_count), neg_large, jnp.float32),
        jnp.zeros((head_count, row_count), jnp.float32),
        jnp.zeros((head_count, row_count, HD), jnp.float32),
    )
    zeros = jnp.zeros((row_count, feat_width), jnp.float32)
    carry = init
    k_piece = lax.all_gather(k_local, "blk", axis=0, tiled=True)
    v_piece = lax.all_gather(v_local, "blk", axis=0, tiled=True)
    piece_len = k_piece.shape[0]
    k_blocks = k_piece.reshape(piece_len // row_count, row_count, feat_width)
    v_blocks = v_piece.reshape(piece_len // row_count, row_count, feat_width)

    def one_block(state, item):
        k_block, v_block, index = item
        live, label = token_meta(index * row_count, row_count, valid, views)
        logits = make_logits(q_local, k_block, own_label, live, label, bias_here)
        top_old, total_old, sums_old = state
        top_new = jnp.maximum(top_old, jnp.max(logits, axis=2))
        expo_vals = jnp.where(live[None, None, :], jnp.exp(logits - top_new[:, :, None]), 0.0)
        factor = jnp.exp(top_old - top_new)
        total_new = total_old * factor + jnp.sum(expo_vals, axis=2)
        added = jnp.einsum(
            "hij,jhd->hid",
            expo_vals.astype(jnp.bfloat16),
            split_heads(v_block, head_count),
            preferred_element_type=jnp.float32,
        )
        return ((top_new, total_new, sums_old * factor[:, :, None] + added), None)

    carry, _ = lax.scan(
        one_block, carry, (k_blocks, v_blocks, jnp.arange(piece_len // row_count, dtype=jnp.int32))
    )
    top_all, total_all, sums_all = carry
    norm_rows = top_all + jnp.log(total_all)
    outputs = sums_all / total_all[:, :, None]
    delta_rows = jnp.einsum(
        "ihd,hid->hi", split_heads(g_local, head_count).astype(jnp.float32), outputs
    )

    def key_step(turn, state):
        k_cur, v_cur, dk_cur, dv_cur, dq_cur = state
        anchor = (cycle_pos - turn) % cycle_size
        live, label = token_meta(anchor * row_count, row_count, valid, views)
        dq_add, dk_add, dv_add = block_grads(
            q_local, g_local, norm_rows, delta_rows, k_cur, v_cur, own_label, live, label, bias_here
        )
        k_next, v_next = shifted((k_cur, v_cur), "blk", 1)
        dk_next, dv_next = shifted((dk_cur + dk_add, dv_cur + dv_add), "blk", 1)
        return (k_next, v_next, dk_next, dv_next, dq_cur + dq_add)

    final = lax.fori_loop(0, cycle_size, key_step, (k_local, v_local, zeros, zeros, zeros))
    dq_total, dk_total, dv_total = (final[4], final[2], final[3])
    grads_back = (dq_total, dk_total, dv_total)
    grad_query, grad_keys, grad_values = (
        lax.all_to_all(grads_back[0], "head", split_axis=0, concat_axis=1, tiled=True),
        lax.all_to_all(grads_back[1], "head", split_axis=0, concat_axis=1, tiled=True),
        lax.all_to_all(grads_back[2], "head", split_axis=0, concat_axis=1, tiled=True),
    )
    return (grad_query, grad_keys, grad_values)


MESH = pl.DeviceIdType.MESH


def fused_kernel(
    n_head,
    pairs,
    tok,
    q_hbm,
    k_hbm,
    v_hbm,
    g_hbm,
    valid_hbm,
    views_hbm,
    bias_hbm,
    out_ref,
    q_ref,
    k_ref,
    v_ref,
    g_ref,
    valid_ref,
    views_ref,
    bias_ref,
    in_sem,
    word_sem,
    sendbuf,
    rbuf,
    obuf,
    w_scr,
    kv_scr,
    kt_scr,
    t_scr,
    ps_scr,
    xsend,
    xrecv,
    own_kv,
    retbuf,
    send_sem,
    recv_sem,
    fsend_sem,
    frecv_sem,
    xsend_sem,
    xrecv_sem,
    rsend_sem,
    rrecv_sem,
):
    fpd = tok // FRAME
    half = pairs * tok
    per_row = n_head // 2
    hpos = lax.axis_index("head")
    me = lax.axis_index("blk") * n_head + hpos
    pair = me // 2
    core = me % 2

    def device(which_pair, which_core):
        return {
            "blk": which_pair // per_row,
            "head": (which_pair % per_row) * 2 + which_core,
        }

    sibling = device(pair, 1 - core)

    def partner(step):
        other, bit = 0, 1
        while bit < pairs:
            other = other + (pair // bit + step // bit) % 2 * bit
            bit *= 2
        return other


    sources = (q_hbm, k_hbm, v_hbm, g_hbm, valid_hbm, views_hbm, bias_hbm)
    targets = (q_ref, k_ref, v_ref, g_ref, valid_ref, views_ref, bias_ref)
    loads = [
        pltpu.make_async_copy(source, target, in_sem.at[i])
        for i, (source, target) in enumerate(zip(sources, targets))
    ]
    for load in loads:
        load.start()

    n_blk = pairs // per_row
    row_pos = pair // per_row
    across = pair + 1 - 2 * (pair % 2)

    def greet(semaphore, which_pair):
        pl.semaphore_signal(
            semaphore, inc=1, device_id=device(which_pair, core), device_id_type=MESH
        )

    barrier = pltpu.get_barrier_semaphore()
    greet(barrier, across)

    @pl.when(row_pos > 0)
    def _():
        greet(barrier, pair - per_row)

    for to in range(per_row, pairs):

        @pl.when(to // per_row > row_pos)
        def _():
            greet(barrier, to)

    pl.semaphore_signal(barrier, inc=1, device_id=sibling, device_id_type=MESH)

    for load in loads[:4]:
        load.wait()

    for j in range(pairs // 2):
        cols = slice(j * 2 * HD, (j + 1) * 2 * HD)
        qq = q_ref[:, cols] * jnp.bfloat16(scale_factor)
        kk = k_ref[:, cols]
        vv = v_ref[:, cols]
        gg = g_ref[:, cols]
        sendbuf[2 * j, 0:tok, :] = jnp.concatenate([kk[:, :HD], vv[:, :HD]], axis=1)
        sendbuf[2 * j, tok:, :] = jnp.concatenate([qq[:, :HD], gg[:, :HD]], axis=1)
        sendbuf[2 * j + 1, 0:tok, :] = jnp.concatenate([kk[:, HD:], vv[:, HD:]], axis=1)
        sendbuf[2 * j + 1, tok:, :] = jnp.concatenate([qq[:, HD:], gg[:, HD:]], axis=1)

    heard = 2 + row_pos * per_row + (2 * n_blk - 2 - row_pos) // n_blk
    pl.semaphore_wait(barrier, heard)

    def out_copy(to):
        return pltpu.make_async_remote_copy(
            src_ref=sendbuf.at[to],
            dst_ref=rbuf.at[pair],
            send_sem=send_sem.at[to],
            recv_sem=recv_sem.at[pair],
            device_id=device(to, core),
            device_id_type=MESH,
        )

    def in_copy(source):
        return pltpu.make_async_remote_copy(
            src_ref=sendbuf.at[source],
            dst_ref=rbuf.at[source],
            send_sem=send_sem.at[source],
            recv_sem=recv_sem.at[source],
            device_id=device(source, core),
            device_id_type=MESH,
        )

    def forward(source):
        return pltpu.make_async_remote_copy(
            src_ref=rbuf.at[source, pl.ds(0, tok)],
            dst_ref=obuf.at[source],
            send_sem=fsend_sem.at[source],
            recv_sem=frecv_sem.at[source],
            device_id=sibling,
            device_id_type=MESH,
        )

    def send_up(base, distance):
        @pl.when(row_pos + distance < n_blk)
        def _():
            out_copy(base + distance * per_row).start()

    def pass_word(turn):
        @pl.when(row_pos > 0)
        def _():
            greet(word_sem.at[turn - 1], pair - per_row)

    pass_word(1)
    for to in reversed(range(pairs - per_row)):

        @pl.when(to // per_row < row_pos)
        def _():
            out_copy(to).start()

    send_up(pair, 1)
    out_copy(across).start()
    rbuf[pair] = sendbuf[pair]
    forward(pair).start()
    for turn in range(1, n_blk):

        @pl.when(row_pos + 1 < n_blk)
        def _():
            pl.semaphore_wait(word_sem.at[turn - 1], 1)

        if turn + 1 < n_blk:
            pass_word(turn + 1)
        send_up(across, turn)
        if turn + 1 < n_blk:
            send_up(pair, turn + 1)

    for load in loads[4:]:
        load.wait()
    bias = bias_ref[pair]
    lanes = per_row * tok
    both = 2 * lanes
    lane = lax.broadcasted_iota(jnp.int32, (8, lanes), 1)
    low = lax.broadcasted_iota(jnp.int32, (lanes, 2 * HD), 1) < HD
    row = lax.broadcasted_iota(jnp.int32, (FRAME, lanes), 0)
    chunks = lanes // FRAME

    def row_at(k):
        upper = row_pos // (n_blk // 2)
        if k < n_blk // 2:
            other, bit = 0, 1
            while bit < n_blk:
                other = other + (row_pos // bit + k // bit) % 2 * bit
                bit *= 2
            return other
        return k + upper * (n_blk - 1 - 2 * k)

    rows_at = [row_at(k) for k in range(n_blk)]

    def signs(k):
        sign_row = jnp.zeros((8, lanes), jnp.float32)
        for c in range(chunks):
            frame = ((rows_at[k] * per_row + c // fpd) * 2 + core) * fpd + c % fpd
            label = views_ref[frame].astype(jnp.float32)
            sign_row = jnp.where(lane // FRAME == c, bias - 2.0 * bias * label, sign_row)
        return sign_row[0:1]

    sign_rows = [signs(k) for k in range(n_blk)]

    def fold(x, op):
        return op(x.reshape(FRAME // 8, 8, lanes), axis=0)

    def low_half(j):
        return slice(j * both, j * both + lanes)

    def high_half(j):
        return slice(j * both + lanes, (j + 1) * both)

    def start_of(part, k):
        return part * half + k * lanes

    def chunk_at(part, k, c):
        return pl.ds(pl.multiple_of(start_of(part, k) + c * FRAME, FRAME), FRAME)

    def over_keys(key_blocks, body, state):
        for part, k in key_blocks:
            owner = core if part == 0 else 1 - core

            def step(c, carry):
                frame = ((rows_at[k] * per_row + c // fpd) * 2 + owner) * fpd + c % fpd
                return body(chunk_at(part, k, c), frame, carry)

            state = lax.fori_loop(0, chunks, step, state, unroll=chunks)
        return state

    def group(key_blocks, query_blocks):
        def mask(at, frame, best):
            view = views_ref[frame].astype(jnp.float32)
            live = row < valid_ref[frame]
            out = []
            for j, b in zip(query_blocks, best):
                x = jnp.where(live, t_scr[at, low_half(j)] + sign_rows[j] * view, neg_large)
                t_scr[at, low_half(j)] = x
                out.append(jnp.maximum(b, fold(x, jnp.max)))
            return tuple(out)

        start = jnp.full((8, lanes), neg_large, jnp.float32)
        tops = over_keys(key_blocks, mask, (start,) * len(query_blocks))
        tops = [jnp.max(t, axis=0, keepdims=True) for t in tops]

        def expo(at, frame, state):
            out = []
            for j, top, (total, delta) in zip(query_blocks, tops, state):
                e = jnp.exp(t_scr[at, low_half(j)] - top)
                t_scr[at, low_half(j)] = e
                out.append(
                    (total + fold(e, jnp.sum), delta + fold(e * t_scr[at, high_half(j)], jnp.sum))
                )
            return tuple(out)

        none = jnp.zeros((8, lanes), jnp.float32)
        sums = over_keys(key_blocks, expo, ((none, none),) * len(query_blocks))
        return [
            (top, jnp.sum(t, axis=0, keepdims=True), jnp.sum(d, axis=0, keepdims=True))
            for top, (t, d) in zip(tops, sums)
        ]

    def scores(kv, w, parts, cols):
        t = lax.dot_general(kv, w, (((1,), (1,)), ((), ())), preferred_element_type=jnp.float32)
        count = t.shape[0] // len(parts)
        for n, first in enumerate(parts):
            t_scr[first : first + count, cols] = t[n * count : (n + 1) * count]

    found = [[] for _ in range(n_blk)]

    def arrive(k):
        for turn in range(per_row):
            source = rows_at[k] * per_row + (pair + turn) % per_row
            if k + turn > 0:
                in_copy(source).wait_recv()
                forward(source).start()

    def keep_keys(part, k, kv):
        kv = kv.reshape(lanes, 2 * HD)
        first = start_of(part, k)
        kv_scr[first : first + lanes, :] = kv
        kt_scr[:, first : first + lanes] = jnp.transpose(kv)[:HD]
        scores(kv, w_scr[0 : (k + 1) * both, :], [first], slice(0, (k + 1) * both))
        for j, stats in enumerate(group([(part, k)], range(k + 1))):
            found[j].append(([(part, k)], stats))

    def stage_own(k):
        base = pl.ds(rows_at[k] * per_row, per_row)
        qg = rbuf[base, tok:, :].reshape(lanes, 2 * HD)
        zero = jnp.zeros_like(qg)
        w_scr[k * both : k * both + lanes, :] = jnp.where(low, qg, zero)
        w_scr[k * both + lanes : (k + 1) * both, :] = jnp.where(low, zero, qg)
        if k > 0:
            w_new = w_scr[k * both : (k + 1) * both, :]
            for part in range(2):
                first = start_of(part, 0)
                old = kv_scr[first : first + k * lanes, :]
                scores(old, w_new, [first], slice(k * both, (k + 1) * both))
            keys = [(part, i) for part in range(2) for i in range(k)]
            found[k].append((keys, group(keys, [k])[0]))
        keep_keys(0, k, rbuf[base, 0:tok, :])

    def stage_other(k):
        for turn in range(per_row):
            forward(rows_at[k] * per_row + turn).wait_recv()
        keep_keys(1, k, obuf[pl.ds(rows_at[k] * per_row, per_row)])

    arrive(0)
    for k in range(n_blk):
        stage_own(k)
        if k + 1 < n_blk:
            arrive(k + 1)
        stage_other(k)

    scales = {}
    deltas = []
    for j in range(n_blk):
        top = functools.reduce(jnp.maximum, [s[0] for _, s in found[j]])
        ratios = [jnp.exp(s[0] - top) for _, s in found[j]]
        inverse = 1.0 / sum(r * s[1] for r, (_, s) in zip(ratios, found[j]))
        deltas.append(sum(r * s[2] for r, (_, s) in zip(ratios, found[j])) * inverse)
        for r, (keys, _) in zip(ratios, found[j]):
            for key in keys:
                scales[key, j] = r * inverse

    pieces = [range(n_blk // 2, n_blk), range(n_blk // 2)]
    wide = n_blk // 2 * lanes

    def low_grads(part, piece):
        for k in piece:

            def grads(c, carry):
                at = chunk_at(part, k, c)
                for j in range(n_blk):
                    w = t_scr[at, low_half(j)] * scales[(part, k), j]
                    ps_scr[at, high_half(j)] = w.astype(jnp.bfloat16)
                    ds = w * (t_scr[at, high_half(j)] - deltas[j])
                    ps_scr[at, low_half(j)] = ds.astype(jnp.bfloat16)
                return carry

            lax.fori_loop(0, chunks, grads, 0, unroll=chunks)

    def kv_grads(part, piece):
        first = start_of(part, piece[0])
        return jnp.dot(
            ps_scr[first : first + wide, :], w_scr[...], preferred_element_type=jnp.float32
        )

    def exchange(n):
        at = pl.ds(n * wide, wide)
        return pltpu.make_async_remote_copy(
            src_ref=xsend.at[at],
            dst_ref=xrecv.at[at],
            send_sem=xsend_sem.at[n],
            recv_sem=xrecv_sem.at[n],
            device_id=sibling,
            device_id_type=MESH,
        )

    for n, piece in enumerate(pieces):
        low_grads(1, piece)
        xsend[n * wide : (n + 1) * wide] = kv_grads(1, piece).astype(jnp.bfloat16)
        exchange(n).start()
    for piece in pieces:
        low_grads(0, piece)

    def join(n, piece):
        for k in piece:
            dq = jnp.dot(kt_scr[...], ps_scr[:, low_half(k)], preferred_element_type=jnp.float32)
            dq = jnp.transpose(dq * scale_factor).reshape(per_row, tok, HD)
            packed = jnp.concatenate([dq[:, : tok // 2], dq[:, tok // 2 :]], axis=2)
            retbuf[pl.ds(rows_at[k] * per_row, per_row), tok:, :] = packed.astype(jnp.bfloat16)
        own_kv[n * wide : (n + 1) * wide] = kv_grads(0, piece)
        exchange(n).wait_recv()
        at = slice(n * wide, (n + 1) * wide)
        dkv = (own_kv[at, :] + xrecv[at, :].astype(jnp.float32)).astype(jnp.bfloat16)
        for i, k in enumerate(piece):
            rows = dkv[i * lanes : (i + 1) * lanes].reshape(per_row, tok, 2 * HD)
            retbuf[pl.ds(rows_at[k] * per_row, per_row), 0:tok, :] = rows
        for k in reversed(piece):
            for turn in range(per_row):
                to = rows_at[k] * per_row + turn
                if k > 0:
                    back(to, pair).start()
                else:

                    @pl.when(to != pair)
                    def _():
                        back(to, pair).start()

    def back(to, slot):
        return pltpu.make_async_remote_copy(
            src_ref=retbuf.at[to],
            dst_ref=out_ref.at[slot],
            send_sem=rsend_sem.at[to],
            recv_sem=rrecv_sem.at[slot],
            device_id=device(to, core),
            device_id_type=MESH,
        )

    for n, piece in enumerate(pieces):
        join(n, piece)
    out_ref[pair] = retbuf[pair]

    for step in range(1, pairs):
        out_copy((pair + step) % pairs).wait_send()
    for step in range(pairs):
        forward((pair + pairs - step) % pairs).wait_send()
    for n in range(2):
        exchange(n).wait_send()
    for step in range(1, pairs):
        source = (pair + pairs - step) % pairs
        back(source, source).wait_recv()
    for step in range(1, pairs):
        back((pair + step) % pairs, pair).wait_send()


def unpack_kernel(pairs, tok, in_ref, dq_ref, dk_ref, dv_ref):
    for j in range(pairs // 2):
        cols = slice(j * 2 * HD, (j + 1) * 2 * HD)
        a = in_ref[2 * j].astype(jnp.float32)
        b = in_ref[2 * j + 1].astype(jnp.float32)
        dk_ref[:, cols] = jnp.concatenate([a[:tok, :HD], b[:tok, :HD]], axis=1)
        dv_ref[:, cols] = jnp.concatenate([a[:tok, HD:], b[:tok, HD:]], axis=1)
        mid = tok // 2
        dq_ref[:mid, cols] = jnp.concatenate([a[tok:, :HD], b[tok:, :HD]], axis=1)
        dq_ref[mid:, cols] = jnp.concatenate([a[tok:, HD:], b[tok:, HD:]], axis=1)


def local_fused(n_head, pairs, *args):
    query, _, _, _, valid, _, cross_bias = args
    tok, width = query.shape
    half = pairs * tok
    vmem = pl.BlockSpec(memory_space=pltpu.VMEM)
    hbm = pl.BlockSpec(memory_space=pltpu.HBM)
    frames = valid.shape[0]
    rows = tok + tok // 2
    dma = pltpu.SemaphoreType.DMA
    packed = pl.pallas_call(
        functools.partial(fused_kernel, n_head, pairs, tok),
        out_shape=jax.ShapeDtypeStruct((pairs, rows, 2 * HD), jnp.bfloat16),
        in_specs=[hbm] * 7,
        out_specs=vmem,
        scratch_shapes=[
            pltpu.VMEM((tok, width), jnp.bfloat16),
            pltpu.VMEM((tok, width), jnp.bfloat16),
            pltpu.VMEM((tok, width), jnp.bfloat16),
            pltpu.VMEM((tok, width), jnp.bfloat16),
            pltpu.SMEM((frames,), jnp.int32),
            pltpu.SMEM((frames,), jnp.int32),
            pltpu.SMEM((cross_bias.shape[0],), jnp.float32),
            dma((7,)),
            pltpu.SemaphoreType.REGULAR((pairs * 2 // n_head - 1,)),
            pltpu.VMEM((pairs, 2 * tok, 2 * HD), jnp.bfloat16),
            pltpu.VMEM((pairs, 2 * tok, 2 * HD), jnp.bfloat16),
            pltpu.VMEM((pairs, tok, 2 * HD), jnp.bfloat16),
            pltpu.VMEM((2 * half, 2 * HD), jnp.bfloat16),
            pltpu.VMEM((2 * half, 2 * HD), jnp.bfloat16),
            pltpu.VMEM((HD, 2 * half), jnp.bfloat16),
            pltpu.VMEM((2 * half, 2 * half), jnp.float32),
            pltpu.VMEM((2 * half, 2 * half), jnp.bfloat16),
            pltpu.VMEM((half, 2 * HD), jnp.bfloat16),
            pltpu.VMEM((half, 2 * HD), jnp.bfloat16),
            pltpu.VMEM((half, 2 * HD), jnp.float32),
            pltpu.VMEM((pairs, rows, 2 * HD), jnp.bfloat16),
            dma((pairs,)),
            dma((pairs,)),
            dma((pairs,)),
            dma((pairs,)),
            dma((2,)),
            dma((2,)),
            dma((pairs,)),
            dma((pairs,)),
        ],
        compiler_params=pltpu.CompilerParams(
            collective_id=0, has_side_effects=True, vmem_limit_bytes=24 * 1024 * 1024
        ),
    )(*[pltpu.with_memory_space_constraint(x, pltpu.HBM) for x in args])
    grad = jax.ShapeDtypeStruct((tok, width), jnp.float32)
    return pl.pallas_call(
        functools.partial(unpack_kernel, pairs, tok),
        out_shape=(grad, grad, grad),
        in_specs=[vmem],
        out_specs=(vmem, vmem, vmem),
        compiler_params=pltpu.CompilerParams(vmem_limit_bytes=4 * 1024 * 1024),
    )(packed)


def solution(mesh):
    rows = P(("grp", "blk", "head"), None)
    n_blk, n_head = mesh.shape["blk"], mesh.shape["head"]

    def local(query, keys, values, grad_out, valid, views, cross_bias):
        args = (query, keys, values, grad_out, valid, views, cross_bias)
        tok, width = query.shape
        pairs = n_blk * n_head // 2
        one_each = n_head == 4 and pairs & (pairs - 1) == 0 and pairs * HD == width and cross_bias.shape[0] == pairs
        if one_each and tok % (2 * FRAME) == 0 and tok * pairs <= 1024:
            return local_fused(n_head, pairs, *args)
        return local_general(*args)

    return jax.shard_map(
        local,
        mesh=mesh,
        in_specs=(rows, rows, rows, rows, P("grp"), P("grp"), P()),
        out_specs=(rows, rows, rows),
        check_vma=False,
    )
```

```python
import functools

import jax
import jax.numpy as jnp
from jax import lax
from jax.experimental import pallas as pl
from jax.experimental.pallas import tpu as pltpu
from jax.sharding import PartitionSpec as P

HD = 64
FRAME = 32


scale_factor = 0.125
neg_large = -1e30


def shifted(x, axis, by):
    peers = lax.axis_size(axis)
    return lax.ppermute(x, axis, [(i, (i + by) % peers) for i in range(peers)])


def token_meta(start, count, valid, views):
    token_ids = start + jnp.arange(count, dtype=jnp.int32)
    frame_ids = token_ids // FRAME
    onehot = frame_ids[:, None] == jnp.arange(valid.shape[0], dtype=jnp.int32)[None, :]
    limits = jnp.sum(jnp.where(onehot, valid[None, :], 0), axis=1)
    labels = jnp.sum(jnp.where(onehot, views[None, :], 0), axis=1)
    return (token_ids % FRAME < limits, labels)


def split_heads(matrix, head_count):
    return matrix.reshape(matrix.shape[0], head_count, matrix.shape[1] // head_count)


def make_logits(q_part, k_part, q_label, k_live, k_label, bias):
    head_count = bias.shape[0]
    raw = jnp.einsum(
        "ihd,jhd->hij",
        split_heads(q_part, head_count),
        split_heads(k_part, head_count),
        preferred_element_type=jnp.float32,
    )
    cross = (q_label[:, None] != k_label[None, :]).astype(jnp.float32)
    raw = raw * scale_factor + bias[:, None, None] * cross[None]
    return jnp.where(k_live[None, None, :], raw, neg_large)


def block_grads(
    q_part, g_part, log_norm, row_delta, k_part, v_part, q_label, k_live, k_label, bias
):
    head_count = bias.shape[0]
    logits = make_logits(q_part, k_part, q_label, k_live, k_label, bias)
    weights = jnp.where(k_live[None, None, :], jnp.exp(logits - log_norm[:, :, None]), 0.0)
    weights_low = weights.astype(jnp.bfloat16)
    g_heads = split_heads(g_part, head_count)
    grad_v = jnp.einsum("hij,ihd->jhd", weights_low, g_heads, preferred_element_type=jnp.float32)
    grad_weights = jnp.einsum(
        "ihd,jhd->hij", g_heads, split_heads(v_part, head_count), preferred_element_type=jnp.float32
    )
    grad_logits = (scale_factor * weights * (grad_weights - row_delta[:, :, None])).astype(
        jnp.bfloat16
    )
    grad_q = jnp.einsum(
        "hij,jhd->ihd",
        grad_logits,
        split_heads(k_part, head_count),
        preferred_element_type=jnp.float32,
    )
    grad_k = jnp.einsum(
        "hij,ihd->jhd",
        grad_logits,
        split_heads(q_part, head_count),
        preferred_element_type=jnp.float32,
    )
    return (
        grad_q.reshape(q_part.shape[0], -1),
        grad_k.reshape(k_part.shape[0], -1),
        grad_v.reshape(k_part.shape[0], -1),
    )


def local_general(query, keys, values, grad_out, valid, views, cross_bias):
    q_local, k_local, v_local, g_local = (
        lax.all_to_all(query, "head", split_axis=1, concat_axis=0, tiled=True),
        lax.all_to_all(keys, "head", split_axis=1, concat_axis=0, tiled=True),
        lax.all_to_all(values, "head", split_axis=1, concat_axis=0, tiled=True),
        lax.all_to_all(grad_out, "head", split_axis=1, concat_axis=0, tiled=True),
    )
    row_count = q_local.shape[0]
    feat_width = q_local.shape[1]
    head_count = feat_width // HD
    cycle_size = lax.axis_size("blk")
    cycle_pos = lax.axis_index("blk")
    head_pos = lax.axis_index("head")
    bias_here = lax.dynamic_slice_in_dim(cross_bias, head_pos * head_count, head_count)
    own_start = cycle_pos * row_count
    own_live, own_label = token_meta(own_start, row_count, valid, views)
    init = (
        jnp.full((head_count, row_count), neg_large, jnp.float32),
        jnp.zeros((head_count, row_count), jnp.float32),
        jnp.zeros((head_count, row_count, HD), jnp.float32),
    )
    zeros = jnp.zeros((row_count, feat_width), jnp.float32)
    carry = init
    k_piece = lax.all_gather(k_local, "blk", axis=0, tiled=True)
    v_piece = lax.all_gather(v_local, "blk", axis=0, tiled=True)
    piece_len = k_piece.shape[0]
    k_blocks = k_piece.reshape(piece_len // row_count, row_count, feat_width)
    v_blocks = v_piece.reshape(piece_len // row_count, row_count, feat_width)

    def one_block(state, item):
        k_block, v_block, index = item
        live, label = token_meta(index * row_count, row_count, valid, views)
        logits = make_logits(q_local, k_block, own_label, live, label, bias_here)
        top_old, total_old, sums_old = state
        top_new = jnp.maximum(top_old, jnp.max(logits, axis=2))
        expo_vals = jnp.where(live[None, None, :], jnp.exp(logits - top_new[:, :, None]), 0.0)
        factor = jnp.exp(top_old - top_new)
        total_new = total_old * factor + jnp.sum(expo_vals, axis=2)
        added = jnp.einsum(
            "hij,jhd->hid",
            expo_vals.astype(jnp.bfloat16),
            split_heads(v_block, head_count),
            preferred_element_type=jnp.float32,
        )
        return ((top_new, total_new, sums_old * factor[:, :, None] + added), None)

    carry, _ = lax.scan(
        one_block, carry, (k_blocks, v_blocks, jnp.arange(piece_len // row_count, dtype=jnp.int32))
    )
    top_all, total_all, sums_all = carry
    norm_rows = top_all + jnp.log(total_all)
    outputs = sums_all / total_all[:, :, None]
    delta_rows = jnp.einsum(
        "ihd,hid->hi", split_heads(g_local, head_count).astype(jnp.float32), outputs
    )

    def key_step(turn, state):
        k_cur, v_cur, dk_cur, dv_cur, dq_cur = state
        anchor = (cycle_pos - turn) % cycle_size
        live, label = token_meta(anchor * row_count, row_count, valid, views)
        dq_add, dk_add, dv_add = block_grads(
            q_local, g_local, norm_rows, delta_rows, k_cur, v_cur, own_label, live, label, bias_here
        )
        k_next, v_next = shifted((k_cur, v_cur), "blk", 1)
        dk_next, dv_next = shifted((dk_cur + dk_add, dv_cur + dv_add), "blk", 1)
        return (k_next, v_next, dk_next, dv_next, dq_cur + dq_add)

    final = lax.fori_loop(0, cycle_size, key_step, (k_local, v_local, zeros, zeros, zeros))
    dq_total, dk_total, dv_total = (final[4], final[2], final[3])
    grads_back = (dq_total, dk_total, dv_total)
    grad_query, grad_keys, grad_values = (
        lax.all_to_all(grads_back[0], "head", split_axis=0, concat_axis=1, tiled=True),
        lax.all_to_all(grads_back[1], "head", split_axis=0, concat_axis=1, tiled=True),
        lax.all_to_all(grads_back[2], "head", split_axis=0, concat_axis=1, tiled=True),
    )
    return (grad_query, grad_keys, grad_values)


MESH = pl.DeviceIdType.MESH


def fused_kernel(
    n_head,
    pairs,
    tok,
    q_hbm,
    k_hbm,
    v_hbm,
    g_hbm,
    valid_hbm,
    views_hbm,
    bias_hbm,
    out_ref,
    q_ref,
    k_ref,
    v_ref,
    g_ref,
    valid_ref,
    views_ref,
    bias_ref,
    in_sem,
    word_sem,
    sendbuf,
    rbuf,
    obuf,
    w_scr,
    kv_scr,
    kt_scr,
    t_scr,
    ps_scr,
    xsend,
    xrecv,
    own_kv,
    retbuf,
    send_sem,
    recv_sem,
    fsend_sem,
    frecv_sem,
    xsend_sem,
    xrecv_sem,
    rsend_sem,
    rrecv_sem,
):
    fpd = tok // FRAME
    half = pairs * tok
    per_row = n_head // 2
    hpos = lax.axis_index("head")
    me = lax.axis_index("blk") * n_head + hpos
    pair = me // 2
    core = me % 2

    def device(which_pair, which_core):
        return {
            "blk": which_pair // per_row,
            "head": (which_pair % per_row) * 2 + which_core,
        }

    sibling = device(pair, 1 - core)

    def partner(step):
        other, bit = 0, 1
        while bit < pairs:
            other = other + (pair // bit + step // bit) % 2 * bit
            bit *= 2
        return other


    sources = (q_hbm, k_hbm, v_hbm, g_hbm, valid_hbm, views_hbm, bias_hbm)
    targets = (q_ref, k_ref, v_ref, g_ref, valid_ref, views_ref, bias_ref)
    loads = [
        pltpu.make_async_copy(source, target, in_sem.at[i])
        for i, (source, target) in enumerate(zip(sources, targets))
    ]
    n_blk = pairs // per_row
    row_pos = pair // per_row
    across = pair + 1 - 2 * (pair % 2)

    def greet(semaphore, which_pair):
        pl.semaphore_signal(
            semaphore, inc=1, device_id=device(which_pair, core), device_id_type=MESH
        )

    barrier = pltpu.get_barrier_semaphore()
    greet(barrier, across)

    @pl.when(row_pos > 0)
    def _():
        greet(barrier, pair - per_row)

    for load in loads:
        load.start()

    for to in range(per_row, pairs):

        @pl.when(to // per_row > row_pos)
        def _():
            greet(barrier, to)

    pl.semaphore_signal(barrier, inc=1, device_id=sibling, device_id_type=MESH)

    for load in loads[:4]:
        load.wait()

    for j in range(pairs // 2):
        cols = slice(j * 2 * HD, (j + 1) * 2 * HD)
        qq = q_ref[:, cols] * jnp.bfloat16(scale_factor)
        kk = k_ref[:, cols]
        vv = v_ref[:, cols]
        gg = g_ref[:, cols]
        sendbuf[2 * j, 0:tok, :] = jnp.concatenate([kk[:, :HD], vv[:, :HD]], axis=1)
        sendbuf[2 * j, tok:, :] = jnp.concatenate([qq[:, :HD], gg[:, :HD]], axis=1)
        sendbuf[2 * j + 1, 0:tok, :] = jnp.concatenate([kk[:, HD:], vv[:, HD:]], axis=1)
        sendbuf[2 * j + 1, tok:, :] = jnp.concatenate([qq[:, HD:], gg[:, HD:]], axis=1)

    heard = 2 + row_pos * per_row + (2 * n_blk - 2 - row_pos) // n_blk
    pl.semaphore_wait(barrier, heard)

    def out_copy(to):
        return pltpu.make_async_remote_copy(
            src_ref=sendbuf.at[to],
            dst_ref=rbuf.at[pair],
            send_sem=send_sem.at[to],
            recv_sem=recv_sem.at[pair],
            device_id=device(to, core),
            device_id_type=MESH,
        )

    def in_copy(source):
        return pltpu.make_async_remote_copy(
            src_ref=sendbuf.at[source],
            dst_ref=rbuf.at[source],
            send_sem=send_sem.at[source],
            recv_sem=recv_sem.at[source],
            device_id=device(source, core),
            device_id_type=MESH,
        )

    def forward(source):
        return pltpu.make_async_remote_copy(
            src_ref=rbuf.at[source, pl.ds(0, tok)],
            dst_ref=obuf.at[source],
            send_sem=fsend_sem.at[source],
            recv_sem=frecv_sem.at[source],
            device_id=sibling,
            device_id_type=MESH,
        )

    def send_up(base, distance):
        @pl.when(row_pos + distance < n_blk)
        def _():
            out_copy(base + distance * per_row).start()

    def pass_word(turn):
        @pl.when(row_pos > 0)
        def _():
            greet(word_sem.at[turn - 1], pair - per_row)

    pass_word(1)
    for to in reversed(range(pairs - per_row)):

        @pl.when(to // per_row < row_pos)
        def _():
            out_copy(to).start()

    send_up(pair, 1)
    out_copy(across).start()
    rbuf[pair] = sendbuf[pair]
    forward(pair).start()
    for turn in range(1, n_blk):

        @pl.when(row_pos + 1 < n_blk)
        def _():
            pl.semaphore_wait(word_sem.at[turn - 1], 1)

        if turn + 1 < n_blk:
            pass_word(turn + 1)
        send_up(across, turn)
        if turn + 1 < n_blk:
            send_up(pair, turn + 1)

    for load in loads[4:]:
        load.wait()
    bias = bias_ref[pair]
    lanes = per_row * tok
    both = 2 * lanes
    lane = lax.broadcasted_iota(jnp.int32, (8, lanes), 1)
    low = lax.broadcasted_iota(jnp.int32, (lanes, 2 * HD), 1) < HD
    row = lax.broadcasted_iota(jnp.int32, (FRAME, lanes), 0)
    chunks = lanes // FRAME

    def row_at(k):
        upper = row_pos // (n_blk // 2)
        if k < n_blk // 2:
            other, bit = 0, 1
            while bit < n_blk:
                other = other + (row_pos // bit + k // bit) % 2 * bit
                bit *= 2
            return other
        return k + upper * (n_blk - 1 - 2 * k)

    rows_at = [row_at(k) for k in range(n_blk)]

    def signs(k):
        sign_row = jnp.zeros((8, lanes), jnp.float32)
        for c in range(chunks):
            frame = ((rows_at[k] * per_row + c // fpd) * 2 + core) * fpd + c % fpd
            label = views_ref[frame].astype(jnp.float32)
            sign_row = jnp.where(lane // FRAME == c, bias - 2.0 * bias * label, sign_row)
        return sign_row[0:1]

    sign_rows = [signs(k) for k in range(n_blk)]

    def fold(x, op):
        return op(x.reshape(FRAME // 8, 8, lanes), axis=0)

    def low_half(j):
        return slice(j * both, j * both + lanes)

    def high_half(j):
        return slice(j * both + lanes, (j + 1) * both)

    def start_of(part, k):
        return part * half + k * lanes

    def chunk_at(part, k, c):
        return pl.ds(pl.multiple_of(start_of(part, k) + c * FRAME, FRAME), FRAME)

    def over_keys(key_blocks, body, state):
        for part, k in key_blocks:
            owner = core if part == 0 else 1 - core

            def step(c, carry):
                frame = ((rows_at[k] * per_row + c // fpd) * 2 + owner) * fpd + c % fpd
                return body(chunk_at(part, k, c), frame, carry)

            state = lax.fori_loop(0, chunks, step, state, unroll=chunks)
        return state

    def group(key_blocks, query_blocks):
        def mask(at, frame, best):
            view = views_ref[frame].astype(jnp.float32)
            live = row < valid_ref[frame]
            out = []
            for j, b in zip(query_blocks, best):
                x = jnp.where(live, t_scr[at, low_half(j)] + sign_rows[j] * view, neg_large)
                t_scr[at, low_half(j)] = x
                out.append(jnp.maximum(b, fold(x, jnp.max)))
            return tuple(out)

        start = jnp.full((8, lanes), neg_large, jnp.float32)
        tops = over_keys(key_blocks, mask, (start,) * len(query_blocks))
        tops = [jnp.max(t, axis=0, keepdims=True) for t in tops]

        def expo(at, frame, state):
            out = []
            for j, top, (total, delta) in zip(query_blocks, tops, state):
                e = jnp.exp(t_scr[at, low_half(j)] - top)
                t_scr[at, low_half(j)] = e
                out.append(
                    (total + fold(e, jnp.sum), delta + fold(e * t_scr[at, high_half(j)], jnp.sum))
                )
            return tuple(out)

        none = jnp.zeros((8, lanes), jnp.float32)
        sums = over_keys(key_blocks, expo, ((none, none),) * len(query_blocks))
        return [
            (top, jnp.sum(t, axis=0, keepdims=True), jnp.sum(d, axis=0, keepdims=True))
            for top, (t, d) in zip(tops, sums)
        ]

    def scores(kv, w, parts, cols):
        t = lax.dot_general(kv, w, (((1,), (1,)), ((), ())), preferred_element_type=jnp.float32)
        count = t.shape[0] // len(parts)
        for n, first in enumerate(parts):
            t_scr[first : first + count, cols] = t[n * count : (n + 1) * count]

    found = [[] for _ in range(n_blk)]

    def arrive(k):
        for turn in range(per_row):
            source = rows_at[k] * per_row + (pair + turn) % per_row
            if k + turn > 0:
                in_copy(source).wait_recv()
                forward(source).start()

    def keep_keys(part, k, kv):
        kv = kv.reshape(lanes, 2 * HD)
        first = start_of(part, k)
        kv_scr[first : first + lanes, :] = kv
        kt_scr[:, first : first + lanes] = jnp.transpose(kv)[:HD]
        scores(kv, w_scr[0 : (k + 1) * both, :], [first], slice(0, (k + 1) * both))
        for j, stats in enumerate(group([(part, k)], range(k + 1))):
            found[j].append(([(part, k)], stats))

    def stage_own(k):
        base = pl.ds(rows_at[k] * per_row, per_row)
        qg = rbuf[base, tok:, :].reshape(lanes, 2 * HD)
        zero = jnp.zeros_like(qg)
        w_scr[k * both : k * both + lanes, :] = jnp.where(low, qg, zero)
        w_scr[k * both + lanes : (k + 1) * both, :] = jnp.where(low, zero, qg)
        if k > 0:
            w_new = w_scr[k * both : (k + 1) * both, :]
            for part in range(2):
                first = start_of(part, 0)
                old = kv_scr[first : first + k * lanes, :]
                scores(old, w_new, [first], slice(k * both, (k + 1) * both))
            keys = [(part, i) for part in range(2) for i in range(k)]
            found[k].append((keys, group(keys, [k])[0]))
        keep_keys(0, k, rbuf[base, 0:tok, :])

    def stage_other(k):
        for turn in range(per_row):
            forward(rows_at[k] * per_row + turn).wait_recv()
        keep_keys(1, k, obuf[pl.ds(rows_at[k] * per_row, per_row)])

    arrive(0)
    for k in range(n_blk):
        stage_own(k)
        if k + 1 < n_blk:
            arrive(k + 1)
        stage_other(k)

    scales = {}
    deltas = []
    for j in range(n_blk):
        top = functools.reduce(jnp.maximum, [s[0] for _, s in found[j]])
        ratios = [jnp.exp(s[0] - top) for _, s in found[j]]
        inverse = 1.0 / sum(r * s[1] for r, (_, s) in zip(ratios, found[j]))
        deltas.append(sum(r * s[2] for r, (_, s) in zip(ratios, found[j])) * inverse)
        for r, (keys, _) in zip(ratios, found[j]):
            for key in keys:
                scales[key, j] = r * inverse

    pieces = [range(n_blk // 2, n_blk), range(n_blk // 2)]
    wide = n_blk // 2 * lanes

    def low_grads(part, piece):
        for k in piece:

            def grads(c, carry):
                at = chunk_at(part, k, c)
                for j in range(n_blk):
                    w = t_scr[at, low_half(j)] * scales[(part, k), j]
                    ps_scr[at, high_half(j)] = w.astype(jnp.bfloat16)
                    ds = w * (t_scr[at, high_half(j)] - deltas[j])
                    ps_scr[at, low_half(j)] = ds.astype(jnp.bfloat16)
                return carry

            lax.fori_loop(0, chunks, grads, 0, unroll=chunks)

    def kv_grads(part, piece):
        first = start_of(part, piece[0])
        return jnp.dot(
            ps_scr[first : first + wide, :], w_scr[...], preferred_element_type=jnp.float32
        )

    def exchange(n):
        at = pl.ds(n * wide, wide)
        return pltpu.make_async_remote_copy(
            src_ref=xsend.at[at],
            dst_ref=xrecv.at[at],
            send_sem=xsend_sem.at[n],
            recv_sem=xrecv_sem.at[n],
            device_id=sibling,
            device_id_type=MESH,
        )

    for n, piece in enumerate(pieces):
        low_grads(1, piece)
        xsend[n * wide : (n + 1) * wide] = kv_grads(1, piece).astype(jnp.bfloat16)
        exchange(n).start()
    for piece in pieces:
        low_grads(0, piece)

    def join(n, piece):
        for k in piece:
            dq = jnp.dot(kt_scr[...], ps_scr[:, low_half(k)], preferred_element_type=jnp.float32)
            dq = jnp.transpose(dq * scale_factor).reshape(per_row, tok, HD)
            packed = jnp.concatenate([dq[:, : tok // 2], dq[:, tok // 2 :]], axis=2)
            retbuf[pl.ds(rows_at[k] * per_row, per_row), tok:, :] = packed.astype(jnp.bfloat16)
        own_kv[n * wide : (n + 1) * wide] = kv_grads(0, piece)
        exchange(n).wait_recv()
        at = slice(n * wide, (n + 1) * wide)
        dkv = (own_kv[at, :] + xrecv[at, :].astype(jnp.float32)).astype(jnp.bfloat16)
        for i, k in enumerate(piece):
            rows = dkv[i * lanes : (i + 1) * lanes].reshape(per_row, tok, 2 * HD)
            retbuf[pl.ds(rows_at[k] * per_row, per_row), 0:tok, :] = rows
        for k in reversed(piece):
            for turn in range(per_row):
                to = rows_at[k] * per_row + turn
                if k > 0:
                    back(to, pair).start()
                else:

                    @pl.when(to != pair)
                    def _():
                        back(to, pair).start()

    def back(to, slot):
        return pltpu.make_async_remote_copy(
            src_ref=retbuf.at[to],
            dst_ref=out_ref.at[slot],
            send_sem=rsend_sem.at[to],
            recv_sem=rrecv_sem.at[slot],
            device_id=device(to, core),
            device_id_type=MESH,
        )

    for n, piece in enumerate(pieces):
        join(n, piece)
    out_ref[pair] = retbuf[pair]

    for step in range(1, pairs):
        out_copy((pair + step) % pairs).wait_send()
    for step in range(pairs):
        forward((pair + pairs - step) % pairs).wait_send()
    for n in range(2):
        exchange(n).wait_send()
    for step in range(1, pairs):
        source = (pair + pairs - step) % pairs
        back(source, source).wait_recv()
    for step in range(1, pairs):
        back((pair + step) % pairs, pair).wait_send()


def unpack_kernel(pairs, tok, in_ref, dq_ref, dk_ref, dv_ref):
    for j in range(pairs // 2):
        cols = slice(j * 2 * HD, (j + 1) * 2 * HD)
        a = in_ref[2 * j].astype(jnp.float32)
        b = in_ref[2 * j + 1].astype(jnp.float32)
        dk_ref[:, cols] = jnp.concatenate([a[:tok, :HD], b[:tok, :HD]], axis=1)
        dv_ref[:, cols] = jnp.concatenate([a[:tok, HD:], b[:tok, HD:]], axis=1)
        mid = tok // 2
        dq_ref[:mid, cols] = jnp.concatenate([a[tok:, :HD], b[tok:, :HD]], axis=1)
        dq_ref[mid:, cols] = jnp.concatenate([a[tok:, HD:], b[tok:, HD:]], axis=1)


def local_fused(n_head, pairs, *args):
    query, _, _, _, valid, _, cross_bias = args
    tok, width = query.shape
    half = pairs * tok
    vmem = pl.BlockSpec(memory_space=pltpu.VMEM)
    hbm = pl.BlockSpec(memory_space=pltpu.HBM)
    frames = valid.shape[0]
    rows = tok + tok // 2
    dma = pltpu.SemaphoreType.DMA
    packed = pl.pallas_call(
        functools.partial(fused_kernel, n_head, pairs, tok),
        out_shape=jax.ShapeDtypeStruct((pairs, rows, 2 * HD), jnp.bfloat16),
        in_specs=[hbm] * 7,
        out_specs=vmem,
        scratch_shapes=[
            pltpu.VMEM((tok, width), jnp.bfloat16),
            pltpu.VMEM((tok, width), jnp.bfloat16),
            pltpu.VMEM((tok, width), jnp.bfloat16),
            pltpu.VMEM((tok, width), jnp.bfloat16),
            pltpu.SMEM((frames,), jnp.int32),
            pltpu.SMEM((frames,), jnp.int32),
            pltpu.SMEM((cross_bias.shape[0],), jnp.float32),
            dma((7,)),
            pltpu.SemaphoreType.REGULAR((pairs * 2 // n_head - 1,)),
            pltpu.VMEM((pairs, 2 * tok, 2 * HD), jnp.bfloat16),
            pltpu.VMEM((pairs, 2 * tok, 2 * HD), jnp.bfloat16),
            pltpu.VMEM((pairs, tok, 2 * HD), jnp.bfloat16),
            pltpu.VMEM((2 * half, 2 * HD), jnp.bfloat16),
            pltpu.VMEM((2 * half, 2 * HD), jnp.bfloat16),
            pltpu.VMEM((HD, 2 * half), jnp.bfloat16),
            pltpu.VMEM((2 * half, 2 * half), jnp.float32),
            pltpu.VMEM((2 * half, 2 * half), jnp.bfloat16),
            pltpu.VMEM((half, 2 * HD), jnp.bfloat16),
            pltpu.VMEM((half, 2 * HD), jnp.bfloat16),
            pltpu.VMEM((half, 2 * HD), jnp.float32),
            pltpu.VMEM((pairs, rows, 2 * HD), jnp.bfloat16),
            dma((pairs,)),
            dma((pairs,)),
            dma((pairs,)),
            dma((pairs,)),
            dma((2,)),
            dma((2,)),
            dma((pairs,)),
            dma((pairs,)),
        ],
        compiler_params=pltpu.CompilerParams(
            collective_id=0, has_side_effects=True, vmem_limit_bytes=24 * 1024 * 1024
        ),
    )(*[pltpu.with_memory_space_constraint(x, pltpu.HBM) for x in args])
    grad = jax.ShapeDtypeStruct((tok, width), jnp.float32)
    return pl.pallas_call(
        functools.partial(unpack_kernel, pairs, tok),
        out_shape=(grad, grad, grad),
        in_specs=[vmem],
        out_specs=(vmem, vmem, vmem),
        compiler_params=pltpu.CompilerParams(vmem_limit_bytes=4 * 1024 * 1024),
    )(packed)


def solution(mesh):
    rows = P(("grp", "blk", "head"), None)
    n_blk, n_head = mesh.shape["blk"], mesh.shape["head"]

    def local(query, keys, values, grad_out, valid, views, cross_bias):
        args = (query, keys, values, grad_out, valid, views, cross_bias)
        tok, width = query.shape
        pairs = n_blk * n_head // 2
        one_each = n_head == 4 and pairs & (pairs - 1) == 0 and pairs * HD == width and cross_bias.shape[0] == pairs
        if one_each and tok % (2 * FRAME) == 0 and tok * pairs <= 1024:
            return local_fused(n_head, pairs, *args)
        return local_general(*args)

    return jax.shard_map(
        local,
        mesh=mesh,
        in_specs=(rows, rows, rows, rows, P("grp"), P("grp"), P()),
        out_specs=(rows, rows, rows),
        check_vma=False,
    )
```
